512 devices in a mesh: req: 128 (over z, y, core), mlp: 4 (over x).
Axes of the slice: x: 4, y: 8, z: 8, core: 2. Of those that a mesh axis runs over, the one named last changes fastest.
Arguments:
- patches: bfloat16 [16384, 4, 1280], P('req', 'mlp'), may hold values from -6 to 6
- vis_gain: float32 [1280], replicated, may hold values from 0.5 to 1.5
- proj_weight: bfloat16 [4, 1280, 1280], P('mlp', 'req'), may hold values from -0.078125 to 0.078125
- image_dest: int32 [16384, 1], P('req'), may hold values from 0 to 127; in each aligned block of 128 rows (0 to 127, 128 to 255, ...) at most 2 rows name the same one
- image_pos: int32 [128], P('req'), may hold values from 0 to 255
- text_len: int32 [128], P('req'), may hold values from 64 to 255
- text: bfloat16 [128, 256, 1280], P('req'), may hold values from -6 to 6
- attn_gain: float32 [1280], replicated, may hold values from 0.5 to 1.5
- qkv_weight: bfloat16 [3, 1280, 1280], P(None, 'req', 'mlp'), may hold values from -0.15625 to 0.15625
- out_weight: bfloat16 [1280, 1280], P('mlp', 'req'), may hold values from -0.15625 to 0.15625
- cache_keys: bfloat16 [128, 1280, 1280], P('req', None, 'mlp')
- cache_values: bfloat16 [128, 1280, 1280], P('req', None, 'mlp'), may hold values from -6 to 6
- held: bfloat16 [16384, 1280], P('req'), may hold values from -6 to 6
- held_owner: int32 [128, 128, 1], P('req'), may hold values from 0 to 127; in each aligned block of 128 rows (0 to 127, 128 to 255, ..., all dimensions but the last counted through in order) at most 2 rows name the same one
- held_row: int32 [128, 128], P('req'), may hold values from 0 to 127
- recompute_pos: int32 [128, 128], P('req'), may hold values from 0 to 1279, as said below
Outputs:
- attended: bfloat16 [128, 256, 1280], P('req', None, 'mlp')
The draws below stay inside these ranges and needn't reach their ends.
Inputs may be any that keep to these rules, and one draw needn't show every extreme that they name: `image_dest`: within each aligned block of 128 rows no request is named more than 2 times. `held_owner`: within each request's 128 rows no owner is named more than 2 times. `recompute_pos`: the positions of one request are distinct.
All inputs are finite; a program needn't handle non-finite values.
Results may differ from the reference program's by a relative error of at most 0.013.
The reference program's roundings to bfloat16 on the way count: a program that leaves them out, or rounds other values in their place, can miss the bound.
Values may be sent and summed in bfloat16 or wider, within the bound.
A program may use at most 128 MiB of HBM per device.

```python
import math
import jax
import jax.numpy as jnp
import numpy as np
from jax import lax

VW = 1280
D = 1280
HEAD_DIM = 80
SEQ = 256
IMG_DEV = 128
CACHE = 1280
HELD_DEV = 128
REQS = 128
IMG_TOTAL = 16384
HELD_TOTAL = 16384
CAP = 2
IMG_MAX = 256
RECOMP = 128
FCAP = 2


def draw_cache_keys(key, part):
    return jax.random.normal(key, (REQS, CACHE, D), jnp.float32).astype(jnp.bfloat16)


def draw_recompute_pos(key, part):
    request_keys = jax.random.split(jax.random.fold_in(key, 11), REQS)
    chosen = jax.vmap(lambda one_key: jax.random.permutation(one_key, CACHE)[:RECOMP])(request_keys)
    return chosen.astype(jnp.int32)


def set_ends(drawn, rng, low, high):
    longest = drawn.shape.index(max(drawn.shape))
    spots = []
    for shift in (0, 1):
        where = [jax.random.randint(jax.random.fold_in(rng, axis), (), 0, length) for axis, length in enumerate(drawn.shape)]
        where[longest] = (where[longest] + shift) % drawn.shape[longest]
        spots.append(tuple(where))
    return drawn.at[spots[0]].set(low).at[spots[1]].set(high)


def levels(key, dims, cuts, least, largest):
    factor_of, own = 1.0, jax.random.fold_in(key, 6)
    for position, blocks in cuts:
        heights = jnp.exp(jax.random.uniform(jax.random.fold_in(own, position), (blocks,), jnp.float32, least / len(cuts), largest / len(cuts)))
        factor_of = factor_of * jnp.repeat(heights, dims[position] // blocks).reshape([-1 if axis == position else 1 for axis in range(len(dims))])
    return factor_of


def routed_block(rng, own, number, rows, number_of, top, most, skew):
    order = jax.random.permutation(rng, number_of)
    crowded, ordinary = portions_of(number_of, rows * top, most, skew, True), portions_of(number_of, rows * top, most, skew, False)
    places = jnp.arange(number_of)

    def named(sizes, offset_by):
        used = int((sizes > 0).sum())
        fixed = max(1, used // 4)
        moved = fixed + (places - fixed + offset_by * (used - fixed)) % max(1, number_of - fixed)
        return jnp.zeros((number_of,), jnp.int32).at[order[jnp.where(places < fixed, places, moved)]].set(jnp.asarray(sizes, jnp.int32))

    sizes = jnp.where(number % 4 == 0, named(crowded, number // 4), named(ordinary, number - number // 4 - 1))
    mixed = jax.random.permutation(jax.random.fold_in(own, 3), number_of)
    giver, receiver = mixed[0:number_of // 2 * 2:2], mixed[1:number_of // 2 * 2:2]
    margin = jnp.minimum(sizes[giver] - 1, most - sizes[receiver]) // 2
    margin = jnp.where((giver == order[0]) | (receiver == order[0]) | (sizes[receiver] == 0), 0, jnp.maximum(margin, 0))
    moved = jax.random.randint(jax.random.fold_in(own, 4), (number_of // 2,), 0, 1 << 20) % (margin + 1)
    sizes = sizes.at[giver].add(-moved).at[receiver].add(moved)
    members = jnp.searchsorted(jnp.cumsum(sizes), jnp.arange(rows * top), side="right").astype(jnp.int32)
    listing = members.reshape(top, rows).T
    listing = listing[jax.random.permutation(jax.random.fold_in(own, 1), rows)]
    offset_by = jax.random.randint(jax.random.fold_in(own, 2), (rows, 1), 0, top)
    return jnp.take_along_axis(listing, (jnp.arange(top)[None, :] + offset_by) % top, axis=1)


def portions_of(number_of, total, limit, slope, full):
    portions = [(1 << 20) // math.isqrt(grade ** slope) + 1 for grade in range(1, number_of + 1)]
    largest = limit if full else min(limit, max(-(-total // number_of), total * portions[0] // sum(portions)))
    least = 1 if total - largest >= number_of - 1 else 0
    counts, spare = [largest] + [least] * (number_of - 1), total - largest - least * (number_of - 1)
    while spare > 0:
        movable = [i for i in range(1, number_of) if counts[i] < largest] or [i for i in range(1, number_of) if counts[i] < limit]
        whole, left = sum([portions[i] for i in movable]), spare
        for i in movable:
            addition = min(limit - counts[i], max(1, left * portions[i] // whole), spare)
            counts[i] = counts[i] + addition
            spare = spare - addition
    return np.array(counts)


def gaussian(own_key, extent, scale, limit, pieces=(), kind=jnp.bfloat16):
    factor_of = levels(own_key, extent, pieces, -0.22, 0.18) if pieces else 1.0
    entries = jax.random.normal(own_key, extent, jnp.float32) * scale * factor_of
    return jnp.minimum(jnp.maximum(entries, -limit), limit).astype(kind)


def setup_inputs(seed: int = 0) -> dict:
    arg_keys = jax.random.split(jax.random.key(seed), 17)
    patches = gaussian(arg_keys[0], (IMG_TOTAL, 4, VW), 1.0, 6.0, ((0, 128), (1, 4)))
    vis_gain = jnp.clip(1.0 + 0.1 * jax.random.normal(arg_keys[1], (VW,), jnp.float32), 0.5, 1.5)
    proj_weight = gaussian(arg_keys[2], (4, VW, D), (4 * VW) ** -0.5, 0.078125, ((0, 4), (1, 128)))
    image_dest_keys = jax.random.split(jax.random.fold_in(arg_keys[3], 1), IMG_TOTAL // IMG_DEV)
    image_dest_turns = jax.random.permutation(jax.random.fold_in(arg_keys[3], 3), IMG_TOTAL // IMG_DEV)
    image_dest = jax.vmap(lambda own, number: routed_block(jax.random.fold_in(arg_keys[3], 2), own, number, IMG_DEV, REQS, 1, CAP, 2))(image_dest_keys, image_dest_turns).reshape((IMG_TOTAL, 1))
    image_pos = set_ends(jax.random.randint(arg_keys[4], (REQS,), 0, SEQ), jax.random.fold_in(arg_keys[4], 1), 0, SEQ - 1).astype(jnp.int32)
    text_len = set_ends(jax.random.randint(arg_keys[5], (REQS,), SEQ // 4, SEQ), jax.random.fold_in(arg_keys[5], 1), SEQ // 4, SEQ - 1).astype(jnp.int32)
    text = gaussian(arg_keys[6], (REQS, SEQ, D), 1.0, 6.0, ((0, 128),))
    attn_gain = jnp.clip(1.0 + 0.1 * jax.random.normal(arg_keys[7], (D,), jnp.float32), 0.5, 1.5)
    qkv_weight = gaussian(arg_keys[8], (3, D, D), D ** -0.5, 0.15625, ((1, 128), (2, 4)))
    out_weight = gaussian(arg_keys[9], (D, D), D ** -0.5, 0.15625, ((0, 4), (1, 128)))
    cache_keys = draw_cache_keys(jax.random.fold_in(arg_keys[16], 71), 0)
    cache_values = gaussian(arg_keys[11], (REQS, CACHE, D), 1.0, 6.0, ((0, 128), (2, 4)))
    held = gaussian(arg_keys[12], (HELD_TOTAL, D), 1.0, 6.0, ((0, 128),))
    held_owner_keys = jax.random.split(jax.random.fold_in(arg_keys[13], 1), REQS * RECOMP // RECOMP)
    held_owner_turns = jax.random.permutation(jax.random.fold_in(arg_keys[13], 3), REQS * RECOMP // RECOMP)
    held_owner = jax.vmap(lambda own, number: routed_block(jax.random.fold_in(arg_keys[13], 2), own, number, RECOMP, REQS, 1, FCAP, 1))(held_owner_keys, held_owner_turns).reshape((REQS, RECOMP, 1))
    held_row = set_ends(jax.random.randint(arg_keys[14], (REQS, RECOMP), 0, HELD_DEV), jax.random.fold_in(arg_keys[14], 1), 0, HELD_DEV - 1).astype(jnp.int32)
    recompute_pos = draw_recompute_pos(jax.random.fold_in(arg_keys[16], 71), 0)
    return dict(patches=patches, vis_gain=vis_gain, proj_weight=proj_weight, image_dest=image_dest, image_pos=image_pos, text_len=text_len, text=text, attn_gain=attn_gain, qkv_weight=qkv_weight, out_weight=out_weight, cache_keys=cache_keys, cache_values=cache_values, held=held, held_owner=held_owner, held_row=held_row, recompute_pos=recompute_pos)


eps = 1e-06
big_negative = -1e+30

def norm_rows(values, gain):
    floats = values.astype(jnp.float32)
    return (floats * lax.rsqrt(lax.optimization_barrier(jnp.mean(floats * floats, -1, keepdims=True)) + eps) * gain).astype(jnp.bfloat16)

def attend(queries, all_keys, all_values, length):
    seq_len = queries.shape[0]
    cache_len = all_keys.shape[0] - seq_len
    head_count = queries.shape[1] // HEAD_DIM
    query_heads = queries.reshape(seq_len, head_count, HEAD_DIM).astype(jnp.float32)
    key_heads = all_keys.reshape(-1, head_count, HEAD_DIM).astype(jnp.float32)
    value_heads = all_values.reshape(-1, head_count, HEAD_DIM).astype(jnp.float32)
    scores = jnp.einsum('qhd,khd->hqk', query_heads, key_heads) * HEAD_DIM ** (-0.5)
    row_ids = jnp.arange(seq_len, dtype=jnp.int32)[:, None]
    col_ids = jnp.arange(all_keys.shape[0], dtype=jnp.int32)[None, :] - cache_len
    allowed = (col_ids < 0) | (col_ids <= row_ids) & (col_ids < length)
    scores = jnp.where(allowed[None], scores, big_negative)
    highest = lax.optimization_barrier(jnp.max(scores, -1, keepdims=True))
    weights = jnp.exp(scores - highest)
    weights = (weights / lax.optimization_barrier(jnp.sum(weights, -1, keepdims=True))).astype(jnp.bfloat16)
    mixed = jnp.einsum('hqk,khd->qhd', weights.astype(jnp.float32), value_heads).astype(jnp.bfloat16)
    mixed = mixed.reshape(seq_len, -1)
    return jnp.where(row_ids < length, mixed, jnp.zeros_like(mixed))

def reference(patches, vis_gain, proj_weight, image_dest, image_pos, text_len, text, attn_gain, qkv_weight, out_weight, cache_keys, cache_values, held, held_owner, held_row, recompute_pos):
    normed_patch = norm_rows(patches, vis_gain).reshape(patches.shape[0], 4 * VW)
    image_tokens = jnp.dot(normed_patch, proj_weight.reshape(4 * VW, D), preferred_element_type=jnp.float32).astype(jnp.bfloat16)
    targets = image_dest[:, 0]

    def one_request(request):
        is_mine = targets == request
        img_count = jnp.sum(is_mine.astype(jnp.int32))
        row_order = jnp.nonzero(is_mine, size=IMG_MAX, fill_value=0)[0].astype(jnp.int32)
        picked = image_tokens[row_order]
        offset = jnp.minimum(image_pos[request], SEQ - img_count)
        spots = jnp.arange(SEQ, dtype=jnp.int32)
        in_image = (spots >= offset) & (spots < offset + img_count)
        image_index = jnp.clip(spots - offset, 0, IMG_MAX - 1)
        text_index = jnp.clip(jnp.where(spots < offset, spots, spots - img_count), 0, SEQ - 1)
        prompt = jnp.where(in_image[:, None], picked[image_index], text[request][text_index])
        length = jnp.minimum(SEQ, text_len[request] + img_count)
        normed = norm_rows(prompt, attn_gain)
        queries = jnp.dot(normed, qkv_weight[0], preferred_element_type=jnp.float32).astype(jnp.bfloat16)
        new_keys = jnp.dot(normed, qkv_weight[1], preferred_element_type=jnp.float32).astype(jnp.bfloat16)
        new_values = jnp.dot(normed, qkv_weight[2], preferred_element_type=jnp.float32).astype(jnp.bfloat16)
        sources = held_owner[request, :, 0] * HELD_DEV + held_row[request]
        held_norm = norm_rows(held[sources], attn_gain)
        fresh_keys = jnp.dot(held_norm, qkv_weight[1], preferred_element_type=jnp.float32).astype(jnp.bfloat16)
        fresh_values = jnp.dot(held_norm, qkv_weight[2], preferred_element_type=jnp.float32).astype(jnp.bfloat16)
        places = recompute_pos[request]
        keys_now = cache_keys[request].at[places].set(fresh_keys)
        values_now = cache_values[request].at[places].set(fresh_values)
        mixed = attend(queries, jnp.concatenate([keys_now, new_keys], 0), jnp.concatenate([values_now, new_values], 0), length)
        return jnp.dot(mixed, out_weight, preferred_element_type=jnp.float32).astype(jnp.bfloat16)
    return lax.map(one_request, jnp.arange(REQS, dtype=jnp.int32))
```

```python
import functools

import jax
import jax.numpy as jnp
import numpy as np
from jax import lax
from jax.experimental import pallas as pl
from jax.experimental.pallas import tpu as pltpu
from jax.sharding import PartitionSpec as P

HEAD_DIM = 80
eps = 1e-06
big_negative = -1e30
MESH = pl.DeviceIdType.MESH
NZ, NY, NC, NX = 8, 8, 2, 4
GROUP = NY * NC
WIDTH = 1280
HALF = WIDTH // 2
SHARD = 10
PIECE = 16
BLOCK = GROUP * SHARD
WINDOW = 384
OFFSETS = (0, 256, 640, 896)
WIDTHS = (256, 384, 256, 384)
ROWS = 256
HEADS = 4
LOCAL = HEADS * HEAD_DIM
f32, bf16 = jnp.float32, jnp.bfloat16


def coords():
    r, m = lax.axis_index("req"), lax.axis_index("mlp")
    return r, m, lax.div(r, GROUP), lax.rem(lax.div(r, NC), NY), lax.rem(r, NC)


def at(z, y, c, m):
    return (z * GROUP + y * NC + c, m)


def send(src, dst, send_sem, recv_sem, device):
    copy = pltpu.make_async_remote_copy(
        src_ref=src,
        dst_ref=dst,
        send_sem=send_sem,
        recv_sem=recv_sem,
        device_id=device,
        device_id_type=MESH,
    )
    copy.start()
    return copy


def arrival(dst, send_sem, recv_sem, device):
    pltpu.make_async_remote_copy(
        src_ref=dst,
        dst_ref=dst,
        send_sem=send_sem,
        recv_sem=recv_sem,
        device_id=device,
        device_id_type=MESH,
    ).wait_recv()


def meet(devices):
    barrier = pltpu.get_barrier_semaphore()
    for device in devices:
        pl.semaphore_signal(barrier, inc=1, device_id=device, device_id_type=MESH)
    pl.semaphore_wait(barrier, len(devices))


def iota(shape, dim):
    return lax.broadcasted_iota(jnp.int32, shape, dim)


def hot(mask):
    return jnp.where(mask, 1.0, 0.0).astype(bf16)


def mm(a, b):
    return jnp.dot(a, b, preferred_element_type=f32)


def mm_t(a, b):
    return lax.dot_general(a, b, (((1,), (1,)), ((), ())), preferred_element_type=f32)


def norm(x, gain):
    scale = lax.rsqrt(jnp.mean(x * x, -1, keepdims=True) + eps)
    return (x * scale * gain).astype(bf16)


def swap_order(rows_first):
    a, b = iota((ROWS, ROWS), 0), iota((ROWS, ROWS), 1)
    if not rows_first:
        a, b = b, a
    other = (a & 7) * 32 + ((a >> 3) & 1) * 16 + (a >> 4)
    return hot(other == b)


class Ring:
    def __init__(self, out, own, half, place, right, left, sibling, sems):
        self.out, self.own, self.half, self.place = out, own, half, place
        self.right, self.left, self.sibling = right, left, sibling
        self.ssem, self.rsem, self.local = sems
        self.sent = []

    def spot(self, half, number, part=None):
        ref = self.out.at[half, lax.rem(number + 2 * NZ, NZ)]
        if part is None:
            return ref
        return ref.at[pl.ds(part * (BLOCK // 2), BLOCK // 2)]

    def push(self, src, dst, slot, device):
        self.sent.append(send(src, dst, self.ssem.at[slot], self.rsem.at[slot], device))

    def start(self):
        dst = self.spot(self.half, self.place)
        self.push(self.own, dst, 0, self.right)
        self.push(self.own, dst, 4, self.left)
        self.push(self.own, dst, 8, self.sibling)
        self.kept = pltpu.make_async_copy(self.own, dst, self.local)
        self.kept.start()

    def step(self, s):
        for side, sign, device, base in ((0, -1, self.right, 0), (1, 1, self.left, 4)):
            number = self.place + sign * (1 + s)
            part = side if s == 3 else None
            got = self.spot(self.half, number, part)
            arrival(got, self.ssem.at[base + s], self.rsem.at[base + s], device)
            if s < 3:
                onward = self.spot(self.half, number, side if s == 2 else None)
                self.push(onward, onward, base + s + 1, device)
            self.push(got, got, 9 + 2 * s + side, self.sibling)

    def finish(self):
        other = 1 - self.half
        slot = 8
        arrival(self.spot(other, self.place), self.ssem.at[slot], self.rsem.at[slot], self.sibling)
        for s in range(4):
            for side, sign in ((0, -1), (1, 1)):
                slot = 9 + 2 * s + side
                got = self.spot(other, self.place + sign * (1 + s), side if s == 3 else None)
                arrival(got, self.ssem.at[slot], self.rsem.at[slot], self.sibling)
        self.kept.wait()


def gather_kernel(
    wa_ref,
    wb_ref,
    idx_ref,
    held_ref,
    dense_ref,
    full_a,
    full_b,
    out_cols,
    held_out,
    table,
    piece_a,
    piece_b,
    stage_a,
    stage_b,
    own_a,
    own_b,
    idx_stage,
    idx_own,
    picked,
    hop,
    turned,
    sem_as,
    sem_ar,
    sem_bs,
    sem_br,
    sem_is,
    sem_ir,
    sem_ts,
    sem_tr,
    sem_hs,
    sem_hr,
    sem_gs,
    sem_gr,
    sem_xs,
    sem_xr,
    sem_ras,
    sem_rar,
    sem_rbs,
    sem_rbr,
    sem_local,
):
    r, m, z, y, c = coords()
    yc = y * NC + c
    sibling = at(z, y, 1 - c, m)
    planes = [(r, lax.rem(m + d, NX)) for d in range(1, NX)]
    turn_y = [lax.rem(y + d, NY) for d in range(NY)]
    turn_z = [lax.rem(z + d, NZ) for d in range(NZ)]
    back_y = [lax.rem(y + NY - d, NY) for d in range(NY)]
    back_z = [lax.rem(z + NZ - d, NZ) for d in range(NZ)]
    peers = [sibling] + planes
    peers += [at(z, turn_y[d], h, m) for d in range(1, NY) for h in range(NC)]
    peers += [at(turn_z[d], y, h, m) for d in range(1, NZ) for h in range(NC)]
    meet(peers)
    sent = []

    idx_stage[pl.ds(pl.multiple_of(z * 8, 8), 8), :] = idx_ref[...]
    for d in range(1, NZ):
        dst = idx_stage.at[pl.ds(pl.multiple_of(z * 8, 8), 8)]
        sent.append(send(idx_ref, dst, sem_is.at[d], sem_ir.at[d], at(turn_z[d], y, c, m)))

    for piece, ref in ((piece_a, wa_ref), (piece_b, wb_ref)):
        for h in range(NC):
            piece[h] = jnp.zeros((PIECE, HALF), bf16)
            piece[h, 0:SHARD, :] = ref[:, h * HALF : (h + 1) * HALF]

    stage_a[z * NC + c] = jnp.where(c == 0, piece_a[0].astype(f32), piece_a[1].astype(f32)).astype(bf16)
    stage_b[yc] = jnp.where(c == 0, piece_b[0].astype(f32), piece_b[1].astype(f32)).astype(bf16)
    spot_a, spot_b = stage_a.at[z * NC + c], stage_b.at[yc]
    sent.append(send(piece_a.at[1 - c], spot_a, sem_as.at[0, 0], sem_ar.at[0, 0], sibling))
    sent.append(send(piece_b.at[1 - c], spot_b, sem_bs.at[0, 0], sem_br.at[0, 0], sibling))
    for d in range(1, NZ):
        for k in range(NC):
            h = c if k == 0 else 1 - c
            sent.append(
                send(piece_a.at[h], spot_a, sem_as.at[d, k], sem_ar.at[d, k], at(turn_z[d], y, h, m))
            )
            sent.append(
                send(piece_b.at[h], spot_b, sem_bs.at[d, k], sem_br.at[d, k], at(z, turn_y[d], h, m))
            )

    for d in range(1, NZ):
        got = idx_stage.at[pl.ds(pl.multiple_of(back_z[d] * 8, 8), 8)]
        arrival(got, sem_is.at[d], sem_ir.at[d], at(back_z[d], y, c, m))
    for which in range(2):
        idx_own[which] = idx_stage[pl.ds(which, NZ, stride=8), :]
    table[yc] = idx_own[...]
    sent.append(send(idx_own, table.at[yc], sem_ts.at[0, 0], sem_tr.at[0, 0], sibling))
    for d in range(1, NY):
        for k in range(NC):
            h = c if k == 0 else 1 - c
            sent.append(
                send(idx_own, table.at[yc], sem_ts.at[d, k], sem_tr.at[d, k], at(z, turn_y[d], h, m))
            )

    ring_a = Ring(
        full_a, own_a, c, y, at(z, turn_y[1], c, m), at(z, back_y[1], c, m), sibling,
        (sem_ras, sem_rar, sem_local.at[0]),
    )
    ring_b = Ring(
        full_b, own_b, c, z, at(turn_z[1], y, c, m), at(back_z[1], y, c, m), sibling,
        (sem_rbs, sem_rbr, sem_local.at[1]),
    )
    arrival(stage_a.at[z * NC + 1 - c], sem_as.at[0, 0], sem_ar.at[0, 0], sibling)
    for d in range(1, NZ):
        for k in range(NC):
            h = c if k == 0 else 1 - c
            arrival(stage_a.at[back_z[d] * NC + h], sem_as.at[d, k], sem_ar.at[d, k], at(back_z[d], y, h, m))
    own_a[...] = mm(dense_ref[...], stage_a[...].reshape(GROUP * PIECE, HALF)).astype(bf16)
    ring_a.start()
    arrival(stage_b.at[y * NC + 1 - c], sem_bs.at[0, 0], sem_br.at[0, 0], sibling)
    for d in range(1, NY):
        for k in range(NC):
            h = c if k == 0 else 1 - c
            arrival(stage_b.at[back_y[d] * NC + h], sem_bs.at[d, k], sem_br.at[d, k], at(z, back_y[d], h, m))
    own_b[...] = mm(dense_ref[...], stage_b[...].reshape(GROUP * PIECE, HALF)).astype(bf16)
    ring_b.start()

    arrival(table.at[y * NC + 1 - c], sem_ts.at[0, 0], sem_tr.at[0, 0], sibling)
    for d in range(1, NY):
        for k in range(NC):
            h = c if k == 0 else 1 - c
            arrival(table.at[back_y[d] * NC + h], sem_ts.at[d, k], sem_tr.at[d, k], at(z, back_y[d], h, m))
    code = table[:, 1]
    mine = (code >> 7) == r
    row = (code & 127).astype(f32)
    lane = iota((GROUP, NZ, 128), 2).astype(f32)
    first = jnp.min(jnp.where(mine, lane, 1000.0), -1, keepdims=True)
    is_first = mine & (lane == first)
    want0 = jnp.sum(jnp.where(is_first, row, 0.0), -1, keepdims=True)
    want1 = jnp.sum(jnp.where(mine, row, 0.0), -1, keepdims=True) - want0
    pick0 = jnp.where(lane == want0, 1.0, 0.0)
    pick1 = jnp.where(lane == want1, 1.0, 0.0)
    pick = jnp.concatenate([pick0, pick1], 1).reshape(ROWS, 128).astype(bf16)
    base = pl.multiple_of(m * 320 - lax.rem(m, 2) * 64, 128)
    picked[...] = mm(pick, held_ref[:, pl.ds(base, WINDOW)]).astype(bf16).reshape(GROUP, 16, WINDOW)
    hop[yc] = picked[yc]
    sent.append(
        send(picked.at[y * NC + 1 - c], hop.at[yc], sem_hs.at[0, 0], sem_hr.at[0, 0], sibling)
    )
    for d in range(1, NY):
        for k in range(NC):
            h = c if k == 0 else 1 - c
            sent.append(
                send(
                    picked.at[turn_y[d] * NC + h], hop.at[yc], sem_hs.at[d, k], sem_hr.at[d, k],
                    at(z, turn_y[d], h, m),
                )
            )

    ring_a.step(0)
    ring_b.step(0)

    arrival(hop.at[y * NC + 1 - c], sem_hs.at[0, 0], sem_hr.at[0, 0], sibling)
    for d in range(1, NY):
        for k in range(NC):
            h = c if k == 0 else 1 - c
            arrival(hop.at[back_y[d] * NC + h], sem_hs.at[d, k], sem_hr.at[d, k], at(z, back_y[d], h, m))
    back = mm(swap_order(False), hop[...].reshape(ROWS, WINDOW)).astype(bf16)
    turned[...] = back.reshape(NZ, 32, WINDOW)
    keep = pltpu.make_async_copy(turned.at[z], held_out.at[m, z], sem_local.at[2])
    keep.start()
    for d in range(1, NZ):
        sent.append(
            send(
                turned.at[turn_z[d]], held_out.at[m, z], sem_gs.at[d], sem_gr.at[d],
                at(turn_z[d], y, c, m),
            )
        )

    ring_a.step(1)
    ring_b.step(1)

    keep.wait()
    for d in range(1, NZ):
        arrival(held_out.at[m, back_z[d]], sem_gs.at[d], sem_gr.at[d], at(back_z[d], y, c, m))
    for d in range(1, NX):
        sent.append(send(held_out.at[m], held_out.at[m], sem_xs.at[0, d], sem_xr.at[0, d], planes[d - 1]))

    for s in range(2, 4):
        ring_a.step(s)
        ring_b.step(s)
    ring_b.finish()

    def columns(plane):
        return full_b.at[1, pl.ds(plane * 2, 2), :, pl.ds(0, WINDOW)]

    for d in range(1, NX):
        other = lax.rem(m + d, NX)
        sent.append(send(columns(other), out_cols.at[m], sem_xs.at[1, d], sem_xr.at[1, d], planes[d - 1]))
    mine_cols = pltpu.make_async_copy(columns(m), out_cols.at[m], sem_local.at[3])
    mine_cols.start()
    ring_a.finish()
    mine_cols.wait()
    for d in range(1, NX):
        other = lax.rem(m + NX - d, NX)
        arrival(held_out.at[other], sem_xs.at[0, d], sem_xr.at[0, d], (r, other))
        arrival(out_cols.at[other], sem_xs.at[1, d], sem_xr.at[1, d], (r, other))
    for copy in sent + ring_a.sent + ring_b.sent:
        copy.wait_send()


def image_kernel(
    patch_ref,
    gain_ref,
    weight_ref,
    dest_col,
    dest_row,
    out,
    part,
    parts,
    picked,
    hop,
    turned,
    sem_ps,
    sem_pr,
    sem_zs,
    sem_zr,
    sem_ys,
    sem_yr,
    sem_xs,
    sem_xr,
):
    r, m, z, y, c = coords()
    yc = y * NC + c
    sibling = at(z, y, 1 - c, m)
    planes = [(r, lax.rem(m + d, NX)) for d in range(1, NX)]
    turn_y = [lax.rem(y + d, NY) for d in range(NY)]
    turn_z = [lax.rem(z + d, NZ) for d in range(NZ)]
    back_y = [lax.rem(y + NY - d, NY) for d in range(NY)]
    back_z = [lax.rem(z + NZ - d, NZ) for d in range(NZ)]
    peers = [sibling] + planes
    peers += [at(z, turn_y[d], h, m) for d in range(1, NY) for h in range(NC)]
    peers += [at(turn_z[d], y, c, m) for d in range(1, NZ)]
    meet(peers)
    sent = []

    normed = norm(patch_ref[...].astype(f32), gain_ref[...])
    k, j = iota((WIDTH, WIDTH), 0), iota((WIDTH, WIDTH), 1)
    jz, jy, ji = lax.div(lax.rem(j, 160), 20), lax.div(j, 160), lax.rem(j, 20)
    order = hot(k == jz * 160 + jy * 20 + ji)
    normed = mm(normed, order).astype(bf16)
    left = mm(normed, weight_ref[0].reshape(WIDTH, HALF))
    right = mm(normed, weight_ref[1].reshape(WIDTH, HALF))
    part[0] = left[:, 0:384]
    part[1] = left[:, 256:640]
    part[2] = right[:, 0:384]
    part[3] = right[:, 256:640]
    for d in range(1, NX):
        other = lax.rem(m + d, NX)
        sent.append(send(part.at[other], parts.at[m], sem_ps.at[d], sem_pr.at[d], planes[d - 1]))

    before = (dest_col[...] == dest_row[...]) & (iota((128, 128), 0) < iota((128, 128), 1))
    rank = jnp.sum(jnp.where(before, 1.0, 0.0), 0, keepdims=True)
    q = iota((ROWS, 128), 0)
    target = (q >> 5) * 16 + (q & 15)
    slot = ((q >> 4) & 1).astype(f32)
    choose = hot((dest_row[...] == target) & (rank == slot))
    turn = swap_order(True)

    total = part[m]
    for d in range(1, NX):
        other = lax.rem(m + NX - d, NX)
        arrival(parts.at[other], sem_ps.at[d], sem_pr.at[d], (r, other))
    for d in range(1, NX):
        total = total + parts[lax.rem(m + NX - d, NX)]
    tokens = total.astype(bf16)
    picked[...] = mm(choose, tokens).astype(bf16).reshape(NZ, 32, WINDOW)
    hop[z] = picked[z]
    for d in range(1, NZ):
        sent.append(
            send(picked.at[turn_z[d]], hop.at[z], sem_zs.at[d], sem_zr.at[d], at(turn_z[d], y, c, m))
        )
    for d in range(1, NZ):
        arrival(hop.at[back_z[d]], sem_zs.at[d], sem_zr.at[d], at(back_z[d], y, c, m))
    turned[...] = mm(turn, hop[...].reshape(ROWS, WINDOW)).astype(bf16).reshape(GROUP, 16, WINDOW)
    out[m, yc] = turned[yc]
    sent.append(
        send(turned.at[y * NC + 1 - c], out.at[m, yc], sem_ys.at[0, 0], sem_yr.at[0, 0], sibling)
    )
    for d in range(1, NY):
        for k in range(NC):
            h = c if k == 0 else 1 - c
            sent.append(
                send(
                    turned.at[turn_y[d] * NC + h], out.at[m, yc], sem_ys.at[d, k], sem_yr.at[d, k],
                    at(z, turn_y[d], h, m),
                )
            )
    arrival(out.at[m, y * NC + 1 - c], sem_ys.at[0, 0], sem_yr.at[0, 0], sibling)
    for d in range(1, NY):
        for k in range(NC):
            h = c if k == 0 else 1 - c
            arrival(out.at[m, back_y[d] * NC + h], sem_ys.at[d, k], sem_yr.at[d, k], at(z, back_y[d], h, m))
    for d in range(1, NX):
        sent.append(send(out.at[m], out.at[m], sem_xs.at[d], sem_xr.at[d], planes[d - 1]))
    for d in range(1, NX):
        other = lax.rem(m + NX - d, NX)
        arrival(out.at[other], sem_xs.at[d], sem_xr.at[d], (r, other))
    for copy in sent:
        copy.wait_send()


def attend_kernel(
    scalars,
    image_ref,
    held_ref,
    table,
    text_ref,
    gain_ref,
    weight_ref,
    out_cols,
    cache_keys,
    cache_values,
    owner_col,
    owner_row,
    place_row,
    result,
    rows,
    normed,
    keys,
    values,
    mixed_all,
    sem_s,
    sem_r,
):
    r, m, z, y, c = coords()
    planes = [(r, lax.rem(m + d, NX)) for d in range(1, NX)]
    meet(planes)

    mine = hot(table[:, 0].reshape(128, 128) == r)
    counts = mm_t(jnp.ones((8, 128), bf16), mine)
    s0, s1 = iota((128, 128), 0), iota((128, 128), 1)
    earlier = hot((s0 & 7) * 16 + (s0 >> 3) < (s1 & 7) * 16 + (s1 >> 3))
    before = mm(counts.astype(bf16), earlier)
    s, a = iota((128, ROWS), 0), iota((128, ROWS), 1)
    spread = hot(((s >> 3) == (a >> 4)) & ((s & 7) == (a & 7)))
    counts_a = mm(counts.astype(bf16), spread)[0:1]
    before_a = mm(before.astype(bf16), spread)[0:1]
    slot = ((iota((1, ROWS), 1) >> 3) & 1).astype(f32)
    number = jnp.sum(counts[0:1], -1, keepdims=True)
    asked = jnp.full((1, 1), scalars[0], jnp.int32).astype(f32)
    text_len = jnp.full((1, 1), scalars[1], jnp.int32).astype(f32)
    start = jnp.minimum(asked, ROWS - number)
    length = jnp.minimum(float(ROWS), text_len + number)
    q = iota((ROWS, ROWS), 0).astype(f32)
    t = iota((ROWS, ROWS), 1).astype(f32)
    choose = hot((before_a + slot == q - start) & (counts_a > slot))
    take = hot(((q < start) & (t == q)) | ((q >= start + number) & (t == q - number)))
    for b in range(NX):
        o, w = OFFSETS[b], WIDTHS[b]
        image = image_ref[b].reshape(ROWS, WINDOW)[:, 0:w]
        rows[0:ROWS, o : o + w] = mm(choose, image) + mm(take, text_ref[:, o : o + w])

    same = (owner_col[...] == owner_row[...]) & (iota((128, 128), 1) < iota((128, 128), 0))
    rank = jnp.sum(jnp.where(same, 1.0, 0.0), -1, keepdims=True).astype(jnp.int32)
    owner = owner_col[...]
    spot = (owner >> 4) * 32 + rank * 16 + (owner & 15)
    fetch = hot(spot == iota((128, ROWS), 1))
    for b in range(NX):
        o, w = OFFSETS[b], WIDTHS[b]
        held = held_ref[b].reshape(ROWS, WINDOW)[:, 0:w]
        rows[ROWS : ROWS + 128, o : o + w] = mm(fetch, held)
    normed[...] = norm(rows[...], gain_ref[...])

    first = weight_ref[0].reshape(WIDTH, HALF)
    second = weight_ref[1].reshape(WIDTH, HALF)
    queries = mm(normed[0:ROWS], first[:, 0:384]).astype(bf16)[:, 0:LOCAL]
    fresh_k = mm(normed[...], first[:, 256:640]).astype(bf16)[:, 64:384]
    fresh_v = mm(normed[...], second[:, 256:640]).astype(bf16)[:, 64:384]
    keys[WIDTH:, :] = fresh_k[0:ROWS]
    values[WIDTH:, :] = fresh_v[0:ROWS]
    fresh_k, fresh_v = fresh_k[ROWS:], fresh_v[ROWS:]
    for b in range(5):
        span = slice(b * 256, (b + 1) * 256)
        match = place_row[...] == iota((256, 128), 0) + b * 256
        put = hot(match)
        hit = jnp.sum(jnp.where(match, 1.0, 0.0), -1, keepdims=True) > 0.0
        keys[span, :] = jnp.where(hit, mm(put, fresh_k), cache_keys[span, :].astype(f32)).astype(bf16)
        values[span, :] = jnp.where(hit, mm(put, fresh_v), cache_values[span, :].astype(f32)).astype(bf16)

    lanes = iota((ROWS, LOCAL), 1)
    seen = (t <= q) & (t < length)
    mixed = jnp.zeros((ROWS, LOCAL), f32)
    for h in range(HEADS):
        inside = (lanes >= h * HEAD_DIM) & (lanes < (h + 1) * HEAD_DIM)
        part = jnp.where(inside, queries.astype(f32), 0.0).astype(bf16)
        scores = mm_t(part, keys[...]) * HEAD_DIM ** (-0.5)
        old, new = scores[:, 0:WIDTH], jnp.where(seen, scores[:, WIDTH:], big_negative)
        highest = jnp.maximum(jnp.max(old, -1, keepdims=True), jnp.max(new, -1, keepdims=True))
        old, new = jnp.exp(old - highest), jnp.exp(new - highest)
        inverse = 1.0 / (jnp.sum(old, -1, keepdims=True) + jnp.sum(new, -1, keepdims=True))
        old, new = (old * inverse).astype(bf16), (new * inverse).astype(bf16)
        summed = mm(old, values[0:WIDTH]) + mm(new, values[WIDTH:])
        mixed = jnp.where(inside, summed, mixed)
    mixed = jnp.where(iota((ROWS, LOCAL), 0).astype(f32) < length, mixed, 0.0)
    mixed_all[m] = mixed.astype(bf16)

    sent = []
    for d in range(1, NX):
        sent.append(send(mixed_all.at[m], mixed_all.at[m], sem_s.at[d], sem_r.at[d], planes[d - 1]))
    terms = mm_t(mixed_all[m], out_cols[m].reshape(LOCAL, WINDOW)[:, 0:LOCAL])
    for d in range(1, NX):
        other = lax.rem(m + NX - d, NX)
        arrival(mixed_all.at[other], sem_s.at[d], sem_r.at[d], (r, other))
        terms = terms + mm_t(mixed_all[other], out_cols[other].reshape(LOCAL, WINDOW)[:, 0:LOCAL])
    result[...] = terms.astype(bf16)
    for copy in sent:
        copy.wait_send()


VM = functools.partial(pl.BlockSpec, memory_space=pltpu.VMEM)
HB = functools.partial(pl.BlockSpec, memory_space=pl.ANY)
SD = jax.ShapeDtypeStruct
DMA = pltpu.SemaphoreType.DMA


def params(number):
    return pltpu.CompilerParams(
        collective_id=number, has_side_effects=True, vmem_limit_bytes=48 * 1024 * 1024
    )


def local(
    patches,
    vis_gain,
    proj_weight,
    image_dest,
    image_pos,
    text_len,
    text,
    attn_gain,
    qkv_weight,
    out_weight,
    cache_keys,
    cache_values,
    held,
    held_owner,
    held_row,
    recompute_pos,
):
    wb = jnp.concatenate([qkv_weight[0], qkv_weight[1], out_weight.T, qkv_weight[2]], 1)
    dest_row = image_dest.reshape(1, 128)
    owner_row = held_owner.reshape(1, 128)
    idx = jnp.concatenate([dest_row, owner_row * 128 + held_row, jnp.zeros((6, 128), jnp.int32)], 0)
    k, p = np.arange(BLOCK)[:, None], np.arange(GROUP * PIECE)[None, :]
    dense = jnp.asarray((p == k // SHARD * PIECE + k % SHARD).astype(np.float32)).astype(bf16)

    full_a, full_b, out_cols, held_rows, table = pl.pallas_call(
        gather_kernel,
        out_shape=(
            SD((2, NY, BLOCK, HALF), bf16),
            SD((2, NZ, BLOCK, HALF), bf16),
            SD((NX, 2, BLOCK, WINDOW), bf16),
            SD((NX, NZ, 32, WINDOW), bf16),
            SD((GROUP, 2, NZ, 128), jnp.int32),
        ),
        in_specs=[VM()] * 5,
        out_specs=(HB(), HB(), HB(), HB(), VM()),
        scratch_shapes=[
            pltpu.VMEM((2, PIECE, HALF), bf16),
            pltpu.VMEM((2, PIECE, HALF), bf16),
            pltpu.VMEM((GROUP, PIECE, HALF), bf16),
            pltpu.VMEM((GROUP, PIECE, HALF), bf16),
            pltpu.VMEM((BLOCK, HALF), bf16),
            pltpu.VMEM((BLOCK, HALF), bf16),
            pltpu.VMEM((64, 128), jnp.int32),
            pltpu.VMEM((2, NZ, 128), jnp.int32),
            pltpu.VMEM((GROUP, 16, WINDOW), bf16),
            pltpu.VMEM((GROUP, 16, WINDOW), bf16),
            pltpu.VMEM((NZ, 32, WINDOW), bf16),
            DMA((NZ, 2)),
            DMA((NZ, 2)),
            DMA((NY, 2)),
            DMA((NY, 2)),
            DMA((NZ,)),
            DMA((NZ,)),
            DMA((NY, 2)),
            DMA((NY, 2)),
            DMA((NY, 2)),
            DMA((NY, 2)),
            DMA((NZ,)),
            DMA((NZ,)),
            DMA((2, NX)),
            DMA((2, NX)),
            DMA((17,)),
            DMA((17,)),
            DMA((17,)),
            DMA((17,)),
            DMA((4,)),
        ],
        compiler_params=params(1),
    )(proj_weight[0], wb, idx, held, dense)

    image_rows = pl.pallas_call(
        image_kernel,
        out_shape=SD((NX, GROUP, 16, WINDOW), bf16),
        in_specs=[VM()] * 5,
        out_specs=VM(),
        scratch_shapes=[
            pltpu.VMEM((NX, 128, WINDOW), f32),
            pltpu.VMEM((NX, 128, WINDOW), f32),
            pltpu.VMEM((NZ, 32, WINDOW), bf16),
            pltpu.VMEM((NZ, 32, WINDOW), bf16),
            pltpu.VMEM((GROUP, 16, WINDOW), bf16),
            DMA((NX,)),
            DMA((NX,)),
            DMA((NZ,)),
            DMA((NZ,)),
            DMA((NY, 2)),
            DMA((NY, 2)),
            DMA((NX,)),
            DMA((NX,)),
        ],
        compiler_params=params(2),
    )(patches[:, 0], vis_gain[None], full_a, image_dest, dest_row)

    scalars = jnp.concatenate([image_pos, text_len])
    result = pl.pallas_call(
        attend_kernel,
        out_shape=SD((ROWS, LOCAL), bf16),
        in_specs=[pl.BlockSpec(memory_space=pltpu.SMEM)] + [VM()] * 12,
        out_specs=VM(),
        scratch_shapes=[
            pltpu.VMEM((ROWS + 128, WIDTH), f32),
            pltpu.VMEM((ROWS + 128, WIDTH), bf16),
            pltpu.VMEM((WIDTH + ROWS, LOCAL), bf16),
            pltpu.VMEM((WIDTH + ROWS, LOCAL), bf16),
            pltpu.VMEM((NX, ROWS, LOCAL), bf16),
            DMA((NX,)),
            DMA((NX,)),
        ],
        compiler_params=params(3),
    )(
        scalars,
        image_rows,
        held_rows,
        table,
        text[0],
        attn_gain[None],
        full_b,
        out_cols,
        cache_keys[0],
        cache_values[0],
        held_owner[0],
        owner_row,
        recompute_pos,
    )
    return result[None]


def solution(mesh):
    in_specs = (
        P("req", "mlp", None),
        P(),
        P("mlp", "req", None),
        P("req", None),
        P("req"),
        P("req"),
        P("req", None, None),
        P(),
        P(None, "req", "mlp"),
        P("mlp", "req"),
        P("req", None, "mlp"),
        P("req", None, "mlp"),
        P("req", None),
        P("req", None, None),
        P("req", None),
        P("req", None),
    )
    out_specs = P("req", None, "mlp")
    return jax.shard_map(local, mesh=mesh, in_specs=in_specs, out_specs=out_specs, check_vma=False)
```

```python
import functools

import jax
import jax.numpy as jnp
import numpy as np
from jax import lax
from jax.experimental import pallas as pl
from jax.experimental.pallas import tpu as pltpu
from jax.sharding import PartitionSpec as P

HEAD_DIM = 80
eps = 1e-06
big_negative = -1e30
MESH = pl.DeviceIdType.MESH
NZ, NY, NC, NX = 8, 8, 2, 4
GROUP = NY * NC
WIDTH = 1280
HALF = WIDTH // 2
SHARD = 10
PIECE = 16
BLOCK = GROUP * SHARD
WINDOW = 384
OFFSETS = (0, 256, 640, 896)
WIDTHS = (256, 384, 256, 384)
ROWS = 256
HEADS = 4
LOCAL = HEADS * HEAD_DIM
f32, bf16 = jnp.float32, jnp.bfloat16


def coords():
    r, m = lax.axis_index("req"), lax.axis_index("mlp")
    return r, m, lax.div(r, GROUP), lax.rem(lax.div(r, NC), NY), lax.rem(r, NC)


def at(z, y, c, m):
    return (z * GROUP + y * NC + c, m)


def send(src, dst, send_sem, recv_sem, device):
    copy = pltpu.make_async_remote_copy(
        src_ref=src,
        dst_ref=dst,
        send_sem=send_sem,
        recv_sem=recv_sem,
        device_id=device,
        device_id_type=MESH,
    )
    copy.start()
    return copy


def arrival(dst, send_sem, recv_sem, device):
    pltpu.make_async_remote_copy(
        src_ref=dst,
        dst_ref=dst,
        send_sem=send_sem,
        recv_sem=recv_sem,
        device_id=device,
        device_id_type=MESH,
    ).wait_recv()


def meet(devices):
    barrier = pltpu.get_barrier_semaphore()
    for device in devices:
        pl.semaphore_signal(barrier, inc=1, device_id=device, device_id_type=MESH)
    pl.semaphore_wait(barrier, len(devices))


def iota(shape, dim):
    return lax.broadcasted_iota(jnp.int32, shape, dim)


def hot(mask):
    return jnp.where(mask, 1.0, 0.0).astype(bf16)


def mm(a, b):
    return jnp.dot(a, b, preferred_element_type=f32)


def mm_t(a, b):
    return lax.dot_general(a, b, (((1,), (1,)), ((), ())), preferred_element_type=f32)


def norm(x, gain):
    scale = lax.rsqrt(jnp.mean(x * x, -1, keepdims=True) + eps)
    return (x * scale * gain).astype(bf16)


def swap_order(rows_first):
    a, b = iota((ROWS, ROWS), 0), iota((ROWS, ROWS), 1)
    if not rows_first:
        a, b = b, a
    other = (a & 7) * 32 + ((a >> 3) & 1) * 16 + (a >> 4)
    return hot(other == b)


class Ring:
    CHUNKS = 5
    ROWS = BLOCK // CHUNKS

    def __init__(self, full, own, c, place, near, sibling, sems):
        self.full, self.own, self.c, self.place = full, own, c, place
        self.near, self.sibling = near, sibling
        self.ssem, self.rsem = sems
        self.sent = []

    def block(self, half, number):
        return self.full.at[half, lax.rem(number + 2 * NZ, NZ)]

    def chunk(self, ref, k):
        return ref.at[pl.ds(k * self.ROWS, self.ROWS)]

    def push(self, src, dst, slot, device):
        self.sent.append(send(src, dst, self.ssem.at[slot], self.rsem.at[slot], device))

    def start(self, value):
        self.full[self.c, self.place] = value
        own = self.block(self.c, self.place)
        for k in range(self.CHUNKS):
            for side in range(2):
                part = self.chunk(own, k)
                self.push(part, part, side * 20 + k, self.near[side])
        self.push(own, own, 40, self.sibling)

    def step(self, s):
        sides = (-1, 1)
        for k in range(self.CHUNKS):
            for side in range(2):
                if s == 3 and (k < 3) != (side == 0):
                    continue
                slot = side * 20 + s * 5 + k
                part = self.chunk(self.block(self.c, self.place + sides[side] * (1 + s)), k)
                arrival(part, self.ssem.at[slot], self.rsem.at[slot], self.near[side])
                if s < 2 or (s == 2 and (k < 3) == (side == 0)):
                    self.push(part, part, slot + 5, self.near[side])
        for side in range(2):
            if s < 3 or side == 0:
                got = self.block(self.c, self.place + sides[side] * (1 + s))
                self.push(got, got, 41 + 2 * s + side, self.sibling)

    def finish(self, place):
        for slot, shift in ((40, 0), (41, -1), (42, 1), (43, -2), (44, 2), (45, -3), (46, 3), (47, -4)):
            got = self.block(1 - self.c, place + shift)
            arrival(got, self.ssem.at[slot], self.rsem.at[slot], self.sibling)


def to_col(row):
    eye = iota((128, 128), 0) == iota((128, 128), 1)
    return jnp.sum(jnp.where(eye, row.astype(f32), 0.0), -1, keepdims=True)


class Pairs:
    def __init__(self, c, sibling, turn, back, device, ssem, rsem, cores=NC):
        self.c, self.sibling, self.turn, self.back = c, sibling, turn, back
        self.device, self.ssem, self.rsem, self.cores = device, ssem, rsem, cores
        self.sent = []

    def spans(self):
        for d in range(1, 8):
            for k in range(self.cores):
                yield d, k, (self.c if k == 0 else 1 - self.c)

    def send(self, pick, dst, own):
        for d, k, h in self.spans():
            to = self.turn[d]
            self.sent.append(
                send(pick(to, h), dst, self.ssem.at[d, k], self.rsem.at[d, k], self.device(to, h))
            )
        if self.cores == 2:
            src = pick(own, 1 - self.c)
            self.sent.append(send(src, dst, self.ssem.at[0, 0], self.rsem.at[0, 0], self.sibling))

    def wait(self, spot, own):
        for d, k, h in self.spans():
            to = self.back[d]
            arrival(spot(to, h), self.ssem.at[d, k], self.rsem.at[d, k], self.device(to, h))
        if self.cores == 2:
            arrival(spot(own, 1 - self.c), self.ssem.at[0, 0], self.rsem.at[0, 0], self.sibling)


def kernel(
    image_pos,
    text_len,
    vis_gain,
    attn_gain,
    wa_hbm,
    wb_hbm,
    dest_hbm,
    owner_hbm,
    row_hbm,
    place_hbm,
    dense_hbm,
    patch_hbm,
    held_hbm,
    text_hbm,
    keys_hbm,
    values_hbm,
    result,
    wa,
    wb,
    small,
    dense,
    patch,
    held,
    text,
    keys,
    values,
    piece,
    stage_a,
    stage_b,
    full_a,
    full_b,
    idx,
    idx_stage,
    idx_own,
    table,
    order,
    normed,
    turned_cols,
    part,
    parts,
    picked_i,
    hop_i,
    turned_i,
    image,
    picked_h,
    hop_h,
    turned_h,
    held_in,
    out_cols,
    rows,
    mixed_all,
    local,
    sem_as,
    sem_ar,
    sem_bs,
    sem_br,
    sem_is,
    sem_ir,
    sem_ts,
    sem_tr,
    sem_hs,
    sem_hr,
    sem_gs,
    sem_gr,
    sem_zs,
    sem_zr,
    sem_ys,
    sem_yr,
    sem_xs,
    sem_xr,
    sem_ras,
    sem_rar,
    sem_rbs,
    sem_rbr,
):
    r, m, z, y, c = coords()
    yc = y * NC + c
    sibling = at(z, y, 1 - c, m)
    planes = [(r, lax.rem(m + d, NX)) for d in range(NX)]
    back_m = [lax.rem(m + NX - d, NX) for d in range(NX)]
    turn_y = [lax.rem(y + d, NY) for d in range(NY)]
    turn_z = [lax.rem(z + d, NZ) for d in range(NZ)]
    back_y = [lax.rem(y + NY - d, NY) for d in range(NY)]
    back_z = [lax.rem(z + NZ - d, NZ) for d in range(NZ)]

    loads = {}
    for number, (name, src, dst) in enumerate(
        (
            ("wa", wa_hbm, wa),
            ("wb", wb_hbm, wb),
            ("dest", dest_hbm, small.at[0]),
            ("owner", owner_hbm, small.at[1]),
            ("row", row_hbm, small.at[2]),
            ("place", place_hbm, small.at[3]),
            ("patch", patch_hbm, patch),
            ("dense", dense_hbm, dense),
            ("held", held_hbm, held),
            ("text", text_hbm, text),
            ("keys", keys_hbm, keys.at[:, pl.ds(0, WIDTH)]),
            ("values", values_hbm, values.at[:, pl.ds(0, WIDTH)]),
        )
    ):
        loads[name] = pltpu.make_async_copy(src, dst, local.at[number])
        loads[name].start()

    peers = [sibling] + planes[1:]
    peers += [at(z, turn_y[d], h, m) for d in range(1, NY) for h in range(NC)]
    peers += [at(turn_z[d], y, h, m) for d in range(1, NZ) for h in range(NC)]
    barrier = pltpu.get_barrier_semaphore()
    for device in peers:
        pl.semaphore_signal(barrier, inc=1, device_id=device, device_id_type=MESH)

    def same_z(p, h):
        return at(z, p, h, m)

    def same_y(p, h):
        return at(p, y, h, m)

    for name in ("wa", "wb", "dest", "owner", "row", "place"):
        loads[name].wait()
    for n, ref in ((0, wa), (1, wb)):
        for h in range(NC):
            piece[n, h] = jnp.zeros((PIECE, HALF), bf16)
            piece[n, h, 0:SHARD, :] = ref[:, h * HALF : (h + 1) * HALF]
    dest_row, owner_row = small[0], small[1]
    idx[...] = jnp.concatenate([dest_row, owner_row * 128 + small[2], jnp.zeros((6, 128), jnp.int32)], 0)
    pl.semaphore_wait(barrier, len(peers))
    sent = []

    mine = pl.ds(pl.multiple_of(z * 8, 8), 8)
    idx_stage[mine, :] = idx[...]
    for d in range(1, NZ):
        sent.append(send(idx, idx_stage.at[mine], sem_is.at[d], sem_ir.at[d], same_y(turn_z[d], c)))

    group = (1 - c) * z + c * y
    back_g = [lax.rem(group + 8 - d, 8) for d in range(8)]

    def spread(n, stage, ssem, rsem):
        kept = jnp.where(c == 0, piece[n, 0].astype(f32), piece[n, 1].astype(f32))
        stage[group * NC + c] = kept.astype(bf16)
        there = (1 - c) * y + c * z
        spot = stage.at[there * NC + c]
        sent.append(send(piece.at[n, 1 - c], spot, ssem.at[0, 0], rsem.at[0, 0], sibling))
        for d in range(1, 8):
            spot = stage.at[z * NC + c]
            sent.append(send(piece.at[n, 0], spot, ssem.at[d, 0], rsem.at[d, c], same_y(turn_z[d], 0)))
            spot = stage.at[y * NC + c]
            sent.append(send(piece.at[n, 1], spot, ssem.at[d, 1], rsem.at[d, c], same_z(turn_y[d], 1)))

    def gathered(stage, ssem, rsem):
        arrival(stage.at[group * NC + 1 - c], ssem.at[0, 0], rsem.at[0, 0], sibling)
        for d in range(1, 8):
            for k in range(NC):
                spot = stage.at[back_g[d] * NC + k]
                arrival(spot, ssem.at[d, 0], rsem.at[d, k], sibling)
        return mm(dense[...], stage[...].reshape(GROUP * PIECE, HALF)).astype(bf16)

    spread(0, stage_a, sem_as, sem_ar)

    loads["patch"].wait()
    xn = norm(patch[...].astype(f32), vis_gain[...].reshape(1, WIDTH))
    j = iota((1, WIDTH), 1)
    source = lax.div(lax.rem(j, 160), 20) * 160 + lax.div(j, 160) * 20 + lax.rem(j, 20)
    for b in range(5):
        span = slice(b * 256, (b + 1) * 256)
        order[span, :] = hot(iota((256, WIDTH), 0) + b * 256 == source)
    normed[0:128, :] = xn
    turned_cols[0:128, :] = mm(xn, order[...]).astype(bf16)

    for d in range(1, NZ):
        got = idx_stage.at[pl.ds(pl.multiple_of(back_z[d] * 8, 8), 8)]
        arrival(got, sem_is.at[d], sem_ir.at[d], same_y(back_z[d], c))
    for which in range(2):
        idx_own[which] = idx_stage[pl.ds(which, NZ, stride=8), :]
    table[yc] = idx_own[...]
    tables = Pairs(c, sibling, turn_y, back_y, same_z, sem_ts, sem_tr)
    tables.send(lambda p, h: idx_own, table.at[yc], y)

    place = (1 - c) * y + c * z
    there = (1 - c) * z + c * y

    def ring_device(p):
        return ((1 - c) * (z * GROUP + p * NC) + c * (p * GROUP + y * NC + 1), m)

    near = [ring_device(lax.rem(place + 1, 8)), ring_device(lax.rem(place + 7, 8))]
    ring_a = Ring(full_a, None, c, place, near, sibling, (sem_ras, sem_rar))
    ring_b = Ring(full_b, None, c, place, near, sibling, (sem_rbs, sem_rbr))
    loads["dense"].wait()
    ring_a.start(gathered(stage_a, sem_as, sem_ar))
    spread(1, stage_b, sem_bs, sem_br)
    ring_a.step(0)

    tables.wait(lambda p, h: table.at[p * NC + h], y)
    code = table[:, 1]
    asked = (code >> 7) == r
    row = (code & 127).astype(f32)
    lane = iota((GROUP, NZ, 128), 2).astype(f32)
    first = jnp.min(jnp.where(asked, lane, 1000.0), -1, keepdims=True)
    want0 = jnp.sum(jnp.where(asked & (lane == first), row, 0.0), -1, keepdims=True)
    want1 = jnp.sum(jnp.where(asked, row, 0.0), -1, keepdims=True) - want0
    pick0 = jnp.where(lane == want0, 1.0, 0.0)
    pick1 = jnp.where(lane == want1, 1.0, 0.0)
    pick = jnp.concatenate([pick0, pick1], 1).reshape(ROWS, 128).astype(bf16)
    base = pl.multiple_of(m * 320 - lax.rem(m, 2) * 64, 128)
    loads["held"].wait()
    picked_h[...] = mm(pick, held[:, pl.ds(base, WINDOW)]).astype(bf16).reshape(GROUP, 16, WINDOW)
    ring_a.step(1)
    hop_h[yc] = picked_h[yc]
    held_y = Pairs(c, sibling, turn_y, back_y, same_z, sem_hs, sem_hr)
    held_y.send(lambda p, h: picked_h.at[p * NC + h], hop_h.at[yc], y)

    own_b = gathered(stage_b, sem_bs, sem_br)
    ring_a.step(2)
    ring_b.start(own_b)
    ring_a.step(3)

    held_y.wait(lambda p, h: hop_h.at[p * NC + h], y)
    back = mm(swap_order(False), hop_h[...].reshape(ROWS, WINDOW)).astype(bf16)
    turned_h[...] = back.reshape(NZ, 32, WINDOW)
    held_in[m, z] = turned_h[z]
    held_z = Pairs(c, sibling, turn_z, back_z, same_y, sem_gs, sem_gr, 1)
    held_z.send(lambda p, h: turned_h.at[p], held_in.at[m, z], z)

    ring_a.finish(there)
    left = mm(turned_cols[0:128, :], full_a[0].reshape(WIDTH, HALF))
    part[0] = left[:, 0:384]
    part[1] = left[:, 256:640]
    right = mm(normed[0:128, :], full_a[1].reshape(WIDTH, HALF))
    part[2] = right[:, 0:384]
    part[3] = right[:, 256:640]
    for d in range(1, NX):
        sent.append(send(part.at[planes[d][1]], parts.at[m], sem_xs.at[0, d], sem_xr.at[0, d], planes[d]))
    ring_b.step(0)

    dest_col = to_col(dest_row)
    earlier = (dest_col == dest_row.astype(f32)) & (iota((128, 128), 0) < iota((128, 128), 1))
    rank = jnp.sum(jnp.where(earlier, 1.0, 0.0), 0, keepdims=True)
    q = iota((ROWS, 128), 0)
    target = (q >> 5) * 16 + (q & 15)
    slot = ((q >> 4) & 1).astype(f32)
    choose = hot((dest_row == target) & (rank == slot))
    turn = swap_order(True)

    held_z.wait(lambda p, h: held_in.at[m, p], z)
    ring_b.step(1)
    total = part[m]
    for d in range(1, NX):
        arrival(parts.at[back_m[d]], sem_xs.at[0, d], sem_xr.at[0, d], (r, back_m[d]))
        total = total + parts[back_m[d]]
    picked_i[...] = mm(choose, total.astype(bf16)).astype(bf16).reshape(NZ, 32, WINDOW)
    hop_i[z] = picked_i[z]
    image_z = Pairs(c, sibling, turn_z, back_z, same_y, sem_zs, sem_zr, 1)
    image_z.send(lambda p, h: picked_i.at[p], hop_i.at[z], z)
    for d in range(1, NX):
        sent.append(send(held_in.at[m], held_in.at[m], sem_xs.at[1, d], sem_xr.at[1, d], planes[d]))
    ring_b.step(2)
    image_z.wait(lambda p, h: hop_i.at[p], z)
    turned_i[...] = mm(turn, hop_i[...].reshape(ROWS, WINDOW)).astype(bf16).reshape(GROUP, 16, WINDOW)
    image[m, yc] = turned_i[yc]
    image_y = Pairs(c, sibling, turn_y, back_y, same_z, sem_ys, sem_yr)
    image_y.send(lambda p, h: turned_i.at[p * NC + h], image.at[m, yc], y)
    ring_b.step(3)
    ring_b.finish(there)
    image_y.wait(lambda p, h: image.at[m, p * NC + h], y)
    for d in range(1, NX):
        sent.append(send(image.at[m], image.at[m], sem_xs.at[2, d], sem_xr.at[2, d], planes[d]))

    def columns(plane):
        return full_b.at[1, pl.ds(plane * 2, 2), :, pl.ds(0, WINDOW)]

    for d in range(1, NX):
        src = columns(planes[d][1])
        sent.append(send(src, out_cols.at[m], sem_xs.at[3, d], sem_xr.at[3, d], planes[d]))
    out_cols[m] = full_b[1, pl.ds(m * 2, 2), :, 0:WINDOW]

    gain = attn_gain[...].reshape(1, WIDTH)
    owner_col = to_col(owner_row)
    same = (owner_col == owner_row.astype(f32)) & (iota((128, 128), 1) < iota((128, 128), 0))
    rank = jnp.sum(jnp.where(same, 1.0, 0.0), -1, keepdims=True).astype(jnp.int32)
    owner = owner_col.astype(jnp.int32)
    spot = (owner >> 4) * 32 + rank * 16 + (owner & 15)
    fetch = hot(spot == iota((128, ROWS), 1))
    for d in range(1, NX):
        arrival(held_in.at[back_m[d]], sem_xs.at[1, d], sem_xr.at[1, d], (r, back_m[d]))
    for b in range(NX):
        o, w = OFFSETS[b], WIDTHS[b]
        rows[0:128, o : o + w] = mm(fetch, held_in[b].reshape(ROWS, WINDOW)[:, 0:w])
    eye = hot(iota((LOCAL, LOCAL), 0) == iota((LOCAL, LOCAL), 1))

    def keys_and_values(count):
        xk = mm(turned_cols[0:count, :], full_b[0].reshape(WIDTH, HALF)[:, 256:640])
        xv = mm(normed[0:count, :], full_b[1].reshape(WIDTH, HALF)[:, 256:640])
        return (
            mm_t(eye, xk.astype(bf16)[:, 64:384]).astype(bf16),
            mm_t(eye, xv.astype(bf16)[:, 64:384]).astype(bf16),
        )

    xn = norm(rows[0:128, :], gain)
    normed[0:128, :] = xn
    turned_cols[0:128, :] = mm(xn, order[...]).astype(bf16)
    fresh = keys_and_values(128)
    loads["keys"].wait()
    loads["values"].wait()
    place_col = to_col(small[3]).astype(jnp.int32)
    for b in range(5):
        span = slice(b * 256, (b + 1) * 256)
        match = place_col == iota((128, 256), 1) + b * 256
        put = hot(match)
        hit = jnp.sum(jnp.where(match, 1.0, 0.0), 0, keepdims=True) > 0.0
        for cached, new in ((keys, fresh[0]), (values, fresh[1])):
            cached[:, span] = jnp.where(hit, mm(new, put), cached[:, span].astype(f32)).astype(bf16)

    named = hot(table[:, 0].reshape(128, 128) == r)
    counts = mm_t(jnp.ones((8, 128), bf16), named)
    s0, s1 = iota((128, 128), 0), iota((128, 128), 1)
    ahead = hot((s0 & 7) * 16 + (s0 >> 3) < (s1 & 7) * 16 + (s1 >> 3))
    before = mm(counts.astype(bf16), ahead)
    s, a = iota((128, ROWS), 0), iota((128, ROWS), 1)
    widen = hot(((s >> 3) == (a >> 4)) & ((s & 7) == (a & 7)))
    counts_a = mm(counts.astype(bf16), widen)[0:1]
    before_a = mm(before.astype(bf16), widen)[0:1]
    slot = ((iota((1, ROWS), 1) >> 3) & 1).astype(f32)
    number = jnp.sum(counts[0:1], -1, keepdims=True)
    wanted = jnp.full((1, 1), image_pos[0], jnp.int32).astype(f32)
    start = jnp.minimum(wanted, ROWS - number)
    length = jnp.minimum(float(ROWS), jnp.full((1, 1), text_len[0], jnp.int32).astype(f32) + number)
    q = iota((ROWS, ROWS), 0).astype(f32)
    t = iota((ROWS, ROWS), 1).astype(f32)
    choose = hot((before_a + slot == q - start) & (counts_a > slot))
    take = hot(((q < start) & (t == q)) | ((q >= start + number) & (t == q - number)))
    loads["text"].wait()
    for b in range(NX):
        o, w = OFFSETS[b], WIDTHS[b]
        rows[:, o : o + w] = mm(take, text[:, o : o + w])
    for d in range(1, NX):
        arrival(image.at[back_m[d]], sem_xs.at[2, d], sem_xr.at[2, d], (r, back_m[d]))
    for b in range(NX):
        o, w = OFFSETS[b], WIDTHS[b]
        rows[:, o : o + w] += mm(choose, image[b].reshape(ROWS, WINDOW)[:, 0:w])

    xn = norm(rows[...], gain)
    normed[...] = xn
    turned_cols[...] = mm(xn, order[...]).astype(bf16)
    queries = mm(turned_cols[...], full_b[0].reshape(WIDTH, HALF)[:, 0:384]).astype(bf16)
    new_keys, new_values = keys_and_values(ROWS)
    keys[:, WIDTH:] = new_keys
    values[:, WIDTH:] = new_values

    factor = HEAD_DIM ** (-0.5) * float(np.log2(np.e))
    for i in range(2):
        span = slice(i * 128, (i + 1) * 128)
        count = 128 * (i + 1)
        qi = iota((128, count), 0) + i * 128
        ti = iota((128, count), 1)
        seen = (ti <= qi) & (ti.astype(f32) < length)
        live = (iota((HEAD_DIM, 128), 1) + i * 128).astype(f32) < length
        for h in range(HEADS):
            lanes = slice(h * HEAD_DIM, (h + 1) * HEAD_DIM)
            head = queries[span, lanes]
            old = mm(head, keys[lanes, 0:WIDTH])
            new = jnp.where(seen, mm(head, keys[lanes, WIDTH : WIDTH + count]), big_negative)
            highest = jnp.maximum(jnp.max(old, -1, keepdims=True), jnp.max(new, -1, keepdims=True))
            old = jnp.exp2((old - highest) * factor)
            new = jnp.exp2((new - highest) * factor)
            inverse = 1.0 / (jnp.sum(old, -1, keepdims=True) + jnp.sum(new, -1, keepdims=True))
            old, new = (old * inverse).astype(bf16), (new * inverse).astype(bf16)
            summed = mm_t(values[lanes, 0:WIDTH], old) + mm_t(values[lanes, WIDTH : WIDTH + count], new)
            mixed_all[m, i, lanes, :] = jnp.where(live, summed, 0.0).astype(bf16)
        for d in range(1, NX):
            half = mixed_all.at[m, i]
            sent.append(send(half, half, sem_xs.at[4 + i, d], sem_xr.at[4 + i, d], planes[d]))

    def product(plane, i):
        return mm(out_cols[plane].reshape(LOCAL, WINDOW)[:, 0:LOCAL], mixed_all[plane, i])

    for d in range(1, NX):
        arrival(out_cols.at[back_m[d]], sem_xs.at[3, d], sem_xr.at[3, d], (r, back_m[d]))
    for i in range(2):
        terms = product(m, i)
        for d in range(1, NX):
            arrival(mixed_all.at[back_m[d], i], sem_xs.at[4 + i, d], sem_xr.at[4 + i, d], (r, back_m[d]))
            terms = terms + product(back_m[d], i)
        result[:, i * 128 : (i + 1) * 128] = terms.astype(bf16)
    for group_sent in (tables, held_y, held_z, image_z, image_y, ring_a, ring_b):
        sent += group_sent.sent
    for copy in sent:
        copy.wait_send()


VM = functools.partial(pl.BlockSpec, memory_space=pltpu.VMEM)
HB = functools.partial(pl.BlockSpec, memory_space=pl.ANY)
SM = functools.partial(pl.BlockSpec, memory_space=pltpu.SMEM)
SD = jax.ShapeDtypeStruct
DMA = pltpu.SemaphoreType.DMA


def local(
    patches,
    vis_gain,
    proj_weight,
    image_dest,
    image_pos,
    text_len,
    text,
    attn_gain,
    qkv_weight,
    out_weight,
    cache_keys,
    cache_values,
    held,
    held_owner,
    held_row,
    recompute_pos,
):
    wb = jnp.concatenate([qkv_weight[0], qkv_weight[1], out_weight.T, qkv_weight[2]], 1)
    k, p = np.arange(BLOCK)[:, None], np.arange(GROUP * PIECE)[None, :]
    dense = jnp.asarray((p == k // SHARD * PIECE + k % SHARD).astype(np.float32)).astype(bf16)
    V = pltpu.VMEM
    result = pl.pallas_call(
        kernel,
        out_shape=SD((LOCAL, ROWS), bf16),
        in_specs=[SM(), SM(), VM(), VM()] + [HB()] * 12,
        out_specs=VM(),
        scratch_shapes=[
            V((SHARD, WIDTH), bf16),
            V((SHARD, WIDTH), bf16),
            V((4, 1, 128), jnp.int32),
            V((BLOCK, GROUP * PIECE), bf16),
            V((128, WIDTH), bf16),
            V((128, WIDTH), bf16),
            V((ROWS, WIDTH), bf16),
            V((LOCAL, WIDTH + ROWS), bf16),
            V((LOCAL, WIDTH + ROWS), bf16),
            V((2, 2, PIECE, HALF), bf16),
            V((GROUP, PIECE, HALF), bf16),
            V((GROUP, PIECE, HALF), bf16),
            V((2, 8, BLOCK, HALF), bf16),
            V((2, 8, BLOCK, HALF), bf16),
            V((8, 128), jnp.int32),
            V((64, 128), jnp.int32),
            V((2, NZ, 128), jnp.int32),
            V((GROUP, 2, NZ, 128), jnp.int32),
            V((WIDTH, WIDTH), bf16),
            V((ROWS, WIDTH), bf16),
            V((ROWS, WIDTH), bf16),
            V((NX, 128, WINDOW), f32),
            V((NX, 128, WINDOW), f32),
            V((NZ, 32, WINDOW), bf16),
            V((NZ, 32, WINDOW), bf16),
            V((GROUP, 16, WINDOW), bf16),
            V((NX, GROUP, 16, WINDOW), bf16),
            V((GROUP, 16, WINDOW), bf16),
            V((GROUP, 16, WINDOW), bf16),
            V((NZ, 32, WINDOW), bf16),
            V((NX, NZ, 32, WINDOW), bf16),
            V((NX, 2, BLOCK, WINDOW), bf16),
            V((ROWS, WIDTH), f32),
            V((NX, 2, LOCAL, 128), bf16),
            DMA((12,)),
            DMA((8, 2)),
            DMA((8, 2)),
            DMA((8, 2)),
            DMA((8, 2)),
            DMA((8,)),
            DMA((8,)),
            DMA((8, 2)),
            DMA((8, 2)),
            DMA((8, 2)),
            DMA((8, 2)),
            DMA((8, 2)),
            DMA((8, 2)),
            DMA((8, 2)),
            DMA((8, 2)),
            DMA((8, 2)),
            DMA((8, 2)),
            DMA((6, NX)),
            DMA((6, NX)),
            DMA((48,)),
            DMA((48,)),
            DMA((48,)),
            DMA((48,)),
        ],
        compiler_params=pltpu.CompilerParams(
            collective_id=1, has_side_effects=True, vmem_limit_bytes=56 * 1024 * 1024
        ),
    )(
        image_pos,
        text_len,
        vis_gain,
        attn_gain,
        proj_weight[0],
        wb,
        image_dest.reshape(1, 128),
        held_owner.reshape(1, 128),
        held_row,
        recompute_pos,
        dense,
        patches[:, 0],
        held,
        text[0],
        cache_keys[0].T,
        cache_values[0].T,
    )
    return result.T[None]


def solution(mesh):
    in_specs = (
        P("req", "mlp", None),
        P(),
        P("mlp", "req", None),
        P("req", None),
        P("req"),
        P("req"),
        P("req", None, None),
        P(),
        P(None, "req", "mlp"),
        P("mlp", "req"),
        P("req", None, "mlp"),
        P("req", None, "mlp"),
        P("req", None),
        P("req", None, None),
        P("req", None),
        P("req", None),
    )
    out_specs = P("req", None, "mlp")
    return jax.shard_map(local, mesh=mesh, in_specs=in_specs, out_specs=out_specs, check_vma=False)
```

```python
import functools

import jax
import jax.numpy as jnp
import numpy as np
from jax import lax
from jax.experimental import pallas as pl
from jax.experimental.pallas import tpu as pltpu
from jax.sharding import PartitionSpec as P

HEAD_DIM = 80
eps = 1e-06
big_negative = -1e30
MESH = pl.DeviceIdType.MESH
NZ, NY, NC, NX = 8, 8, 2, 4
GROUP = NY * NC
WIDTH = 1280
HALF = WIDTH // 2
SHARD = 10
PIECE = 16
BLOCK = GROUP * SHARD
WINDOW = 384
CHUNKS = 3
FIRST = (0, 2, 5, 7)
OFFSETS = (0, 256, 640, 896)
WIDTHS = (256, 384, 256, 384)
ROWS = 256
HEADS = 4
LOCAL = HEADS * HEAD_DIM
f32, bf16 = jnp.float32, jnp.bfloat16


def coords():
    r, m = lax.axis_index("req"), lax.axis_index("mlp")
    return r, m, lax.div(r, GROUP), lax.rem(lax.div(r, NC), NY), lax.rem(r, NC)


def at(z, y, c, m):
    return (z * GROUP + y * NC + c, m)


def send(src, dst, send_sem, recv_sem, device):
    copy = pltpu.make_async_remote_copy(
        src_ref=src,
        dst_ref=dst,
        send_sem=send_sem,
        recv_sem=recv_sem,
        device_id=device,
        device_id_type=MESH,
    )
    copy.start()
    return copy


def arrival(dst, send_sem, recv_sem, device):
    pltpu.make_async_remote_copy(
        src_ref=dst,
        dst_ref=dst,
        send_sem=send_sem,
        recv_sem=recv_sem,
        device_id=device,
        device_id_type=MESH,
    ).wait_recv()


def meet(devices):
    barrier = pltpu.get_barrier_semaphore()
    for device in devices:
        pl.semaphore_signal(barrier, inc=1, device_id=device, device_id_type=MESH)
    pl.semaphore_wait(barrier, len(devices))


def iota(shape, dim):
    return lax.broadcasted_iota(jnp.int32, shape, dim)


def hot(mask):
    return jnp.where(mask, 1.0, 0.0).astype(bf16)


def mm(a, b):
    return jnp.dot(a, b, preferred_element_type=f32)


def mm_t(a, b):
    return lax.dot_general(a, b, (((1,), (1,)), ((), ())), preferred_element_type=f32)


def norm(x, gain):
    scale = lax.rsqrt(jnp.mean(x * x, -1, keepdims=True) + eps)
    return (x * scale * gain).astype(bf16)


def swap_order(rows_first):
    a, b = iota((ROWS, ROWS), 0), iota((ROWS, ROWS), 1)
    if not rows_first:
        a, b = b, a
    other = (a & 7) * 32 + ((a >> 3) & 1) * 16 + (a >> 4)
    return hot(other == b)


class Ring:
    CHUNKS = 5
    ROWS = BLOCK // CHUNKS

    def __init__(self, full, own, c, place, near, sibling, sems):
        self.full, self.own, self.c, self.place = full, own, c, place
        self.near, self.sibling = near, sibling
        self.ssem, self.rsem = sems
        self.sent = []

    def block(self, half, number):
        return self.full.at[half, lax.rem(number + 2 * NZ, NZ)]

    def chunk(self, ref, k):
        return ref.at[pl.ds(k * self.ROWS, self.ROWS)]

    def push(self, src, dst, slot, device):
        self.sent.append(send(src, dst, self.ssem.at[slot], self.rsem.at[slot], device))

    def start(self, value):
        self.full[self.c, self.place] = value
        own = self.block(self.c, self.place)
        for k in range(self.CHUNKS):
            for side in range(2):
                part = self.chunk(own, k)
                self.push(part, part, side * 20 + k, self.near[side])
        self.push(own, own, 40, self.sibling)

    def step(self, s):
        sides = (-1, 1)
        for k in range(self.CHUNKS):
            for side in range(2):
                if s == 3 and (k < 3) != (side == 0):
                    continue
                slot = side * 20 + s * 5 + k
                part = self.chunk(self.block(self.c, self.place + sides[side] * (1 + s)), k)
                arrival(part, self.ssem.at[slot], self.rsem.at[slot], self.near[side])
                if s < 2 or (s == 2 and (k < 3) == (side == 0)):
                    self.push(part, part, slot + 5, self.near[side])
        for side in range(2):
            if s < 3 or side == 0:
                got = self.block(self.c, self.place + sides[side] * (1 + s))
                self.push(got, got, 41 + 2 * s + side, self.sibling)

    def finish(self, place):
        for slot, shift in ((40, 0), (41, -1), (42, 1), (43, -2), (44, 2), (45, -3), (46, 3), (47, -4)):
            got = self.block(1 - self.c, place + shift)
            arrival(got, self.ssem.at[slot], self.rsem.at[slot], self.sibling)


def to_col(row):
    eye = iota((128, 128), 0) == iota((128, 128), 1)
    return jnp.sum(jnp.where(eye, row.astype(f32), 0.0), -1, keepdims=True)


class Pairs:
    def __init__(self, c, sibling, turn, back, device, ssem, rsem, cores=NC):
        self.c, self.sibling, self.turn, self.back = c, sibling, turn, back
        self.device, self.ssem, self.rsem, self.cores = device, ssem, rsem, cores
        self.sent = []

    def spans(self):
        for d in range(1, 8):
            for k in range(self.cores):
                yield d, k, (self.c if k == 0 else 1 - self.c)

    def send(self, pick, dst, own, distances=range(8)):
        for d, k, h in self.spans():
            if d not in distances:
                continue
            to = self.turn[d]
            self.sent.append(
                send(pick(to, h), dst, self.ssem.at[d, k], self.rsem.at[d, k], self.device(to, h))
            )
        if self.cores == 2 and 0 in distances:
            src = pick(own, 1 - self.c)
            self.sent.append(send(src, dst, self.ssem.at[0, 0], self.rsem.at[0, 0], self.sibling))

    def wait(self, spot, own):
        for d, k, h in self.spans():
            to = self.back[d]
            arrival(spot(to, h), self.ssem.at[d, k], self.rsem.at[d, k], self.device(to, h))
        if self.cores == 2:
            arrival(spot(own, 1 - self.c), self.ssem.at[0, 0], self.rsem.at[0, 0], self.sibling)


def kernel(
    image_pos,
    text_len,
    vis_gain,
    attn_gain,
    wa_hbm,
    wb_hbm,
    dest_hbm,
    owner_hbm,
    row_hbm,
    place_hbm,
    patch_hbm,
    held_hbm,
    text_hbm,
    keys_hbm,
    values_hbm,
    result,
    wa,
    wb,
    small,
    dense,
    patch,
    held,
    text,
    keys,
    values,
    piece,
    stage_a,
    stage_b,
    full_a,
    full_b,
    idx,
    idx_stage,
    idx_own,
    table,
    order,
    ordered,
    normed,
    turned_cols,
    part,
    parts,
    picked_i,
    hop_i,
    turned_i,
    image,
    picked_h,
    hop_h,
    turned_h,
    hop_back,
    held_in,
    rows,
    mixed,
    product,
    shares,
    others,
    local,
    sem_as,
    sem_ar,
    sem_bs,
    sem_br,
    sem_is,
    sem_ir,
    sem_ts,
    sem_tr,
    sem_hs,
    sem_hr,
    sem_gs,
    sem_gr,
    sem_zs,
    sem_zr,
    sem_ys,
    sem_yr,
    sem_ps,
    sem_pr,
    sem_qs,
    sem_qr,
    sem_xs,
    sem_xr,
    sem_ras,
    sem_rar,
    sem_rbs,
    sem_rbr,
):
    r, m, z, y, c = coords()
    yc = y * NC + c
    sibling = at(z, y, 1 - c, m)
    planes = [(r, lax.rem(m + d, NX)) for d in range(NX)]
    back_m = [lax.rem(m + NX - d, NX) for d in range(NX)]
    turn_y = [lax.rem(y + d, NY) for d in range(NY)]
    turn_z = [lax.rem(z + d, NZ) for d in range(NZ)]
    back_y = [lax.rem(y + NY - d, NY) for d in range(NY)]
    back_z = [lax.rem(z + NZ - d, NZ) for d in range(NZ)]

    loads = {}
    for number, (name, src, dst) in enumerate(
        (
            ("wa", wa_hbm, wa),
            ("wb", wb_hbm, wb),
            ("dest", dest_hbm, small.at[0]),
            ("owner", owner_hbm, small.at[1]),
            ("row", row_hbm, small.at[2]),
            ("place", place_hbm, small.at[3]),
            ("patch", patch_hbm, patch),
            ("held", held_hbm, held),
            ("text", text_hbm, text),
            ("keys", keys_hbm, keys.at[:, pl.ds(0, WIDTH)]),
            ("values", values_hbm, values.at[:, pl.ds(0, WIDTH)]),
        )
    ):
        loads[name] = pltpu.make_async_copy(src, dst, local.at[number])
        loads[name].start()

    peers = [sibling] + planes[1:]
    peers += [at(z, turn_y[d], h, m) for d in range(1, NY) for h in range(NC)]
    peers += [at(turn_z[d], y, h, m) for d in range(1, NZ) for h in range(NC)]
    barrier = pltpu.get_barrier_semaphore()
    for device in peers:
        pl.semaphore_signal(barrier, inc=1, device_id=device, device_id_type=MESH)

    def same_z(p, h):
        return at(z, p, h, m)

    def same_y(p, h):
        return at(p, y, h, m)

    for name in ("wa", "wb", "dest", "owner", "row", "place"):
        loads[name].wait()
    for n, ref in ((0, wa), (1, wb)):
        for h in range(NC):
            piece[n, h] = jnp.zeros((PIECE, HALF), bf16)
            piece[n, h, 0:SHARD, :] = ref[:, h * HALF : (h + 1) * HALF]
    dest_row, owner_row = small[0], small[1]
    idx[...] = jnp.concatenate([dest_row, owner_row * 128 + small[2], jnp.zeros((6, 128), jnp.int32)], 0)
    pl.semaphore_wait(barrier, len(peers))
    sent = []

    mine = pl.ds(pl.multiple_of(z * 8, 8), 8)
    idx_stage[mine, :] = idx[...]
    for d in range(1, NZ):
        sent.append(send(idx, idx_stage.at[mine], sem_is.at[d], sem_ir.at[d], same_y(turn_z[d], c)))

    group = (1 - c) * z + c * y
    back_g = [lax.rem(group + 8 - d, 8) for d in range(8)]

    def spread(n, stage, ssem, rsem):
        kept = jnp.where(c == 0, piece[n, 0].astype(f32), piece[n, 1].astype(f32))
        stage[group * NC + c] = kept.astype(bf16)
        there = (1 - c) * y + c * z
        spot = stage.at[there * NC + c]
        sent.append(send(piece.at[n, 1 - c], spot, ssem.at[0, 0], rsem.at[0, 0], sibling))
        for d in range(1, 8):
            spot = stage.at[z * NC + c]
            sent.append(send(piece.at[n, 0], spot, ssem.at[d, 0], rsem.at[d, c], same_y(turn_z[d], 0)))
            spot = stage.at[y * NC + c]
            sent.append(send(piece.at[n, 1], spot, ssem.at[d, 1], rsem.at[d, c], same_z(turn_y[d], 1)))

    def gathered(stage, ssem, rsem):
        arrival(stage.at[group * NC + 1 - c], ssem.at[0, 0], rsem.at[0, 0], sibling)
        for d in range(1, 8):
            for k in range(NC):
                spot = stage.at[back_g[d] * NC + k]
                arrival(spot, ssem.at[d, 0], rsem.at[d, k], sibling)
        return mm(dense[...], stage[...].reshape(GROUP * PIECE, HALF)).astype(bf16)

    spread(0, stage_a, sem_as, sem_ar)
    spread(1, stage_b, sem_bs, sem_br)

    loads["patch"].wait()
    xn = norm(patch[...].astype(f32), vis_gain[...].reshape(1, WIDTH))
    j = iota((1, WIDTH), 1)
    source = lax.div(lax.rem(j, 160), 20) * 160 + lax.div(j, 160) * 20 + lax.rem(j, 20)
    for b in range(5):
        span = slice(b * 256, (b + 1) * 256)
        order[span, :] = hot(iota((256, WIDTH), 0) + b * 256 == source)
    normed[0:128, :] = xn
    turned_cols[...] = mm(xn, order[...]).astype(bf16)
    k = iota((BLOCK, 1), 0)
    dense[...] = hot(iota((BLOCK, GROUP * PIECE), 1) == lax.div(k, SHARD) * PIECE + lax.rem(k, SHARD))

    for d in range(1, NZ):
        got = idx_stage.at[pl.ds(pl.multiple_of(back_z[d] * 8, 8), 8)]
        arrival(got, sem_is.at[d], sem_ir.at[d], same_y(back_z[d], c))
    for which in range(2):
        idx_own[which] = idx_stage[pl.ds(which, NZ, stride=8), :]
    place = (1 - c) * y + c * z
    there = (1 - c) * z + c * y

    def ring_device(p):
        return ((1 - c) * (z * GROUP + p * NC) + c * (p * GROUP + y * NC + 1), m)

    near = [ring_device(lax.rem(place + 1, 8)), ring_device(lax.rem(place + 7, 8))]
    ring_a = Ring(full_a, None, c, place, near, sibling, (sem_ras, sem_rar))
    ring_b = Ring(full_b, None, c, place, near, sibling, (sem_rbs, sem_rbr))
    tables = []
    for n in range(2):
        table[n, yc] = idx_own[n]
        tables.append(Pairs(c, sibling, turn_y, back_y, same_z, sem_ts.at[n], sem_tr.at[n]))
    tables[1].send(lambda p, h: idx_own.at[1], table.at[1, yc], y)
    ring_a.start(gathered(stage_a, sem_as, sem_ar))
    ring_a.step(0)

    tables[1].wait(lambda p, h: table.at[1, p * NC + h], y)
    code = table[1]
    asked = (code >> 7) == r
    row = (code & 127).astype(f32)
    lane = iota((GROUP, NZ, 128), 2).astype(f32)
    first = jnp.min(jnp.where(asked, lane, 1000.0), -1, keepdims=True)
    want0 = jnp.sum(jnp.where(asked & (lane == first), row, 0.0), -1, keepdims=True)
    want1 = jnp.sum(jnp.where(asked, row, 0.0), -1, keepdims=True) - want0
    pick0 = jnp.where(lane == want0, 1.0, 0.0)
    pick1 = jnp.where(lane == want1, 1.0, 0.0)
    pick = jnp.concatenate([pick0, pick1], 1).reshape(ROWS, 128).astype(bf16)
    base = pl.multiple_of(m * 320 - lax.rem(m, 2) * 64, 128)
    loads["held"].wait()
    picked_h[...] = mm(pick, held[:, pl.ds(base, WINDOW)]).astype(bf16).reshape(GROUP, 16, WINDOW)
    hop_h[yc] = picked_h[yc]
    held_y = Pairs(c, sibling, turn_y, back_y, same_z, sem_hs, sem_hr)
    for step, distances in ((1, (0, 1, 2)), (2, (3, 4, 5)), (3, (6, 7))):
        held_y.send(lambda p, h: picked_h.at[p * NC + h], hop_h.at[yc], y, distances)
        ring_a.step(step)
    ring_b.start(gathered(stage_b, sem_bs, sem_br))

    ring_a.finish(there)
    left = mm(turned_cols[...], full_a[0].reshape(WIDTH, HALF))
    for b in range(5):
        part[b] = left[:, b * 128 : (b + 1) * 128]
    right = mm(normed[0:128, :], full_a[1].reshape(WIDTH, HALF))
    for b in range(5):
        part[5 + b] = right[:, b * 128 : (b + 1) * 128]
    for k in range(CHUNKS):
        for d in range(1, NX):
            src = part.at[lax.div(planes[d][1] * 5, 2) + k]
            sent.append(send(src, parts.at[m, k], sem_ps.at[k, d], sem_pr.at[k, d], planes[d]))

    dest_col = to_col(dest_row)
    earlier = (dest_col == dest_row.astype(f32)) & (iota((128, 128), 0) < iota((128, 128), 1))
    rank = jnp.sum(jnp.where(earlier, 1.0, 0.0), 0, keepdims=True)
    q = iota((ROWS, 128), 0)
    target = (q >> 5) * 16 + (q & 15)
    slot = ((q >> 4) & 1).astype(f32)
    choose = hot((dest_row == target) & (rank == slot))
    turn = swap_order(True)
    image_z = [Pairs(c, sibling, turn_z, back_z, same_y, sem_zs.at[k], sem_zr.at[k], 1) for k in range(CHUNKS)]
    image_y = [Pairs(c, sibling, turn_y, back_y, same_z, sem_ys.at[k], sem_yr.at[k]) for k in range(CHUNKS)]

    def summed_over_planes(k):
        total = part[lax.div(m * 5, 2) + k]
        for d in range(1, NX):
            arrival(parts.at[back_m[d], k], sem_ps.at[k, d], sem_pr.at[k, d], (r, back_m[d]))
            total = total + parts[back_m[d], k]
        picked_i[k] = mm(choose, total.astype(bf16)).astype(bf16).reshape(NZ, 32, 128)
        hop_i[k, z] = picked_i[k, z]
        image_z[k].send(lambda p, h: picked_i.at[k, p], hop_i.at[k, z], z)

    def along_y(k):
        image_z[k].wait(lambda p, h: hop_i.at[k, p], z)
        turned_i[k] = mm(turn, hop_i[k].reshape(ROWS, 128)).astype(bf16).reshape(GROUP, 16, 128)
        image[m, k, yc] = turned_i[k, yc]
        image_y[k].send(lambda p, h: turned_i.at[k, p * NC + h], image.at[m, k, yc], y)

    def over_planes(k):
        image_y[k].wait(lambda p, h: image.at[m, k, p * NC + h], y)
        for d in range(1, NX):
            own = image.at[m, k]
            sent.append(send(own, own, sem_qs.at[k, d], sem_qr.at[k, d], planes[d]))

    owner_col = to_col(owner_row)
    same = (owner_col == owner_row.astype(f32)) & (iota((128, 128), 1) < iota((128, 128), 0))
    rank = jnp.sum(jnp.where(same, 1.0, 0.0), -1, keepdims=True).astype(jnp.int32)
    owner = owner_col.astype(jnp.int32)
    spot = (owner >> 4) * 32 + rank * 16 + (owner & 15)
    fetch = hot(spot == iota((128, ROWS), 1))
    held_y.wait(lambda p, h: hop_h.at[p * NC + h], y)
    back = mm(swap_order(False), hop_h[...].reshape(ROWS, WINDOW)).astype(bf16)
    turned_h[...] = back.reshape(NZ, 32, WINDOW)
    hop_back[z] = turned_h[z]
    held_z = Pairs(c, sibling, turn_z, back_z, same_y, sem_gs, sem_gr, 1)
    held_z.send(lambda p, h: turned_h.at[p], hop_back.at[z], z)
    ring_b.step(0)
    summed_over_planes(0)
    summed_over_planes(1)
    ring_b.step(1)
    along_y(0)
    summed_over_planes(2)
    held_z.wait(lambda p, h: hop_back.at[p], z)
    held_in[m] = mm(fetch, hop_back[...].reshape(ROWS, WINDOW)).astype(bf16)
    for d in range(1, NX):
        sent.append(send(held_in.at[m], held_in.at[m], sem_xs.at[1, d], sem_xr.at[1, d], planes[d]))
    ring_b.step(2)
    along_y(1)
    ring_b.step(3)
    over_planes(0)
    along_y(2)
    tables[0].send(lambda p, h: idx_own.at[0], table.at[0, yc], y)
    over_planes(1)
    ring_b.finish(there)
    for b in range(5):
        span = slice(b * 256, (b + 1) * 256)
        ordered[span, :] = mm(order[span, :], full_b[0].reshape(WIDTH, HALF)).astype(bf16)
    over_planes(2)

    gain = attn_gain[...].reshape(1, WIDTH)
    for d in range(1, NX):
        arrival(held_in.at[back_m[d]], sem_xs.at[1, d], sem_xr.at[1, d], (r, back_m[d]))
    for b in range(NX):
        o, w = OFFSETS[b], WIDTHS[b]
        rows[0:128, o : o + w] = held_in[b][:, 0:w].astype(f32)
    eye = hot(iota((LOCAL, LOCAL), 0) == iota((LOCAL, LOCAL), 1))

    def keys_and_values(count):
        xk = mm(normed[0:count, :], ordered[:, 256:640])
        xv = mm(normed[0:count, :], full_b[1].reshape(WIDTH, HALF)[:, 256:640])
        return (
            mm_t(eye, xk.astype(bf16)[:, 64:384]).astype(bf16),
            mm_t(eye, xv.astype(bf16)[:, 64:384]).astype(bf16),
        )

    normed[0:128, :] = norm(rows[0:128, :], gain)
    fresh = keys_and_values(128)
    loads["keys"].wait()
    loads["values"].wait()
    place_col = to_col(small[3]).astype(jnp.int32)
    for b in range(5):
        span = slice(b * 256, (b + 1) * 256)
        match = place_col == iota((128, 256), 1) + b * 256
        put = hot(match)
        hit = jnp.sum(jnp.where(match, 1.0, 0.0), 0, keepdims=True) > 0.0
        for cached, new in ((keys, fresh[0]), (values, fresh[1])):
            cached[:, span] = jnp.where(hit, mm(new, put), cached[:, span].astype(f32)).astype(bf16)

    tables[0].wait(lambda p, h: table.at[0, p * NC + h], y)
    named = hot(table[0].reshape(128, 128) == r)
    counts = mm_t(jnp.ones((8, 128), bf16), named)
    s0, s1 = iota((128, 128), 0), iota((128, 128), 1)
    ahead = hot((s0 & 7) * 16 + (s0 >> 3) < (s1 & 7) * 16 + (s1 >> 3))
    before = mm(counts.astype(bf16), ahead)
    s, a = iota((128, ROWS), 0), iota((128, ROWS), 1)
    widen = hot(((s >> 3) == (a >> 4)) & ((s & 7) == (a & 7)))
    counts_a = mm(counts.astype(bf16), widen)[0:1]
    before_a = mm(before.astype(bf16), widen)[0:1]
    slot = ((iota((1, ROWS), 1) >> 3) & 1).astype(f32)
    number = jnp.sum(counts[0:1], -1, keepdims=True)
    wanted = jnp.full((1, 1), image_pos[0], jnp.int32).astype(f32)
    start = jnp.minimum(wanted, ROWS - number)
    length = jnp.minimum(float(ROWS), jnp.full((1, 1), text_len[0], jnp.int32).astype(f32) + number)
    q = iota((ROWS, ROWS), 0).astype(f32)
    t = iota((ROWS, ROWS), 1).astype(f32)
    choose = hot((before_a + slot == q - start) & (counts_a > slot))
    take = hot(((q < start) & (t == q)) | ((q >= start + number) & (t == q - number)))
    loads["text"].wait()
    for b in range(NX):
        o, w = OFFSETS[b], WIDTHS[b]
        rows[:, o : o + w] = mm(take, text[:, o : o + w])
    for k in range(CHUNKS):
        for d in range(1, NX):
            arrival(image.at[back_m[d], k], sem_qs.at[k, d], sem_qr.at[k, d], (r, back_m[d]))
        for b in range(NX):
            if k * 128 < WIDTHS[b]:
                lanes = slice((FIRST[b] + k) * 128, (FIRST[b] + k + 1) * 128)
                rows[:, lanes] += mm(choose, image[b, k].reshape(ROWS, 128))

    normed[...] = norm(rows[...], gain)
    queries = mm(normed[...], ordered[:, 0:384]).astype(bf16)
    new_keys, new_values = keys_and_values(ROWS)
    keys[:, WIDTH:] = new_keys
    values[:, WIDTH:] = new_values

    factor = HEAD_DIM ** (-0.5) * float(np.log2(np.e))
    for i in range(2):
        span = slice(i * 128, (i + 1) * 128)
        count = 128 * (i + 1)
        qi = iota((128, count), 0) + i * 128
        ti = iota((128, count), 1)
        seen = (ti <= qi) & (ti.astype(f32) < length)
        live = (iota((HEAD_DIM, 128), 1) + i * 128).astype(f32) < length
        for h in range(HEADS):
            lanes = slice(h * HEAD_DIM, (h + 1) * HEAD_DIM)
            head = queries[span, lanes]
            old = mm(head, keys[lanes, 0:WIDTH])
            new = jnp.where(seen, mm(head, keys[lanes, WIDTH : WIDTH + count]), big_negative)
            highest = jnp.maximum(jnp.max(old, -1, keepdims=True), jnp.max(new, -1, keepdims=True))
            old = jnp.exp2((old - highest) * factor)
            new = jnp.exp2((new - highest) * factor)
            inverse = 1.0 / (jnp.sum(old, -1, keepdims=True) + jnp.sum(new, -1, keepdims=True))
            old, new = (old * inverse).astype(bf16), (new * inverse).astype(bf16)
            summed = mm_t(values[lanes, 0:WIDTH], old) + mm_t(values[lanes, WIDTH : WIDTH + count], new)
            mixed[i, lanes, :] = jnp.where(live, summed, 0.0).astype(bf16)
        terms = mm(full_b[1].reshape(WIDTH, HALF)[:, 0:LOCAL], mixed[i])
        product[i] = terms.reshape(NX, LOCAL, 128)
        shares[i] = terms.astype(bf16).reshape(NX, LOCAL, 128)
        for d in range(1, NX):
            src, dst = shares.at[i, planes[d][1]], others.at[i, m]
            sent.append(send(src, dst, sem_xs.at[4 + i, d], sem_xr.at[4 + i, d], planes[d]))

    for i in range(2):
        total = product[i, m]
        for d in range(1, NX):
            arrival(others.at[i, back_m[d]], sem_xs.at[4 + i, d], sem_xr.at[4 + i, d], (r, back_m[d]))
            total = total + others[i, back_m[d]].astype(f32)
        result[:, i * 128 : (i + 1) * 128] = total.astype(bf16)
    for group_sent in (*tables, held_y, held_z, *image_z, *image_y, ring_a, ring_b):
        sent += group_sent.sent
    for copy in sent:
        copy.wait_send()


VM = functools.partial(pl.BlockSpec, memory_space=pltpu.VMEM)
HB = functools.partial(pl.BlockSpec, memory_space=pl.ANY)
SM = functools.partial(pl.BlockSpec, memory_space=pltpu.SMEM)
SD = jax.ShapeDtypeStruct
DMA = pltpu.SemaphoreType.DMA


def local(
    patches,
    vis_gain,
    proj_weight,
    image_dest,
    image_pos,
    text_len,
    text,
    attn_gain,
    qkv_weight,
    out_weight,
    cache_keys,
    cache_values,
    held,
    held_owner,
    held_row,
    recompute_pos,
):
    wb = jnp.concatenate([qkv_weight[0], qkv_weight[1], out_weight.T, qkv_weight[2]], 1)
    V = pltpu.VMEM
    result = pl.pallas_call(
        kernel,
        out_shape=SD((LOCAL, ROWS), bf16),
        in_specs=[SM(), SM(), VM(), VM()] + [HB()] * 11,
        out_specs=VM(),
        scratch_shapes=[
            V((SHARD, WIDTH), bf16),
            V((SHARD, WIDTH), bf16),
            V((4, 1, 128), jnp.int32),
            V((BLOCK, GROUP * PIECE), bf16),
            V((128, WIDTH), bf16),
            V((128, WIDTH), bf16),
            V((ROWS, WIDTH), bf16),
            V((LOCAL, WIDTH + ROWS), bf16),
            V((LOCAL, WIDTH + ROWS), bf16),
            V((2, 2, PIECE, HALF), bf16),
            V((GROUP, PIECE, HALF), bf16),
            V((GROUP, PIECE, HALF), bf16),
            V((2, 8, BLOCK, HALF), bf16),
            V((2, 8, BLOCK, HALF), bf16),
            V((8, 128), jnp.int32),
            V((64, 128), jnp.int32),
            V((2, NZ, 128), jnp.int32),
            V((2, GROUP, NZ, 128), jnp.int32),
            V((WIDTH, WIDTH), bf16),
            V((WIDTH, HALF), bf16),
            V((ROWS, WIDTH), bf16),
            V((128, WIDTH), bf16),
            V((10, 128, 128), f32),
            V((NX, CHUNKS, 128, 128), f32),
            V((CHUNKS, NZ, 32, 128), bf16),
            V((CHUNKS, NZ, 32, 128), bf16),
            V((CHUNKS, GROUP, 16, 128), bf16),
            V((NX, CHUNKS, GROUP, 16, 128), bf16),
            V((GROUP, 16, WINDOW), bf16),
            V((GROUP, 16, WINDOW), bf16),
            V((NZ, 32, WINDOW), bf16),
            V((NZ, 32, WINDOW), bf16),
            V((NX, 128, WINDOW), bf16),
            V((ROWS, WIDTH), f32),
            V((2, LOCAL, 128), bf16),
            V((2, NX, LOCAL, 128), f32),
            V((2, NX, LOCAL, 128), bf16),
            V((2, NX, LOCAL, 128), bf16),
            DMA((11,)),
            DMA((8, 2)),
            DMA((8, 2)),
            DMA((8, 2)),
            DMA((8, 2)),
            DMA((8,)),
            DMA((8,)),
            DMA((2, 8, 2)),
            DMA((2, 8, 2)),
            DMA((8, 2)),
            DMA((8, 2)),
            DMA((8, 2)),
            DMA((8, 2)),
            DMA((CHUNKS, 8, 2)),
            DMA((CHUNKS, 8, 2)),
            DMA((CHUNKS, 8, 2)),
            DMA((CHUNKS, 8, 2)),
            DMA((CHUNKS, NX)),
            DMA((CHUNKS, NX)),
            DMA((CHUNKS, NX)),
            DMA((CHUNKS, NX)),
            DMA((8, NX)),
            DMA((8, NX)),
            DMA((48,)),
            DMA((48,)),
            DMA((48,)),
            DMA((48,)),
        ],
        compiler_params=pltpu.CompilerParams(
            collective_id=1, has_side_effects=True, vmem_limit_bytes=56 * 1024 * 1024
        ),
    )(
        image_pos,
        text_len,
        vis_gain,
        attn_gain,
        proj_weight[0],
        wb,
        image_dest.reshape(1, 128),
        held_owner.reshape(1, 128),
        held_row,
        recompute_pos,
        patches[:, 0],
        held,
        text[0],
        cache_keys[0].T,
        cache_values[0].T,
    )
    return result.T[None]


def solution(mesh):
    in_specs = (
        P("req", "mlp", None),
        P(),
        P("mlp", "req", None),
        P("req", None),
        P("req"),
        P("req"),
        P("req", None, None),
        P(),
        P(None, "req", "mlp"),
        P("mlp", "req"),
        P("req", None, "mlp"),
        P("req", None, "mlp"),
        P("req", None),
        P("req", None, None),
        P("req", None),
        P("req", None),
    )
    out_specs = P("req", None, "mlp")
    return jax.shard_map(local, mesh=mesh, in_specs=in_specs, out_specs=out_specs, check_vma=False)
```

```python
import functools

import jax
import jax.numpy as jnp
import numpy as np
from jax import lax
from jax.experimental import pallas as pl
from jax.experimental.pallas import tpu as pltpu
from jax.sharding import PartitionSpec as P

HEAD_DIM = 80
eps = 1e-06
big_negative = -1e30
MESH = pl.DeviceIdType.MESH
NZ, NY, NC, NX = 8, 8, 2, 4
GROUP = NY * NC
WIDTH = 1280
HALF = WIDTH // 2
SHARD = 10
PIECE = 16
BLOCK = GROUP * SHARD
WINDOW = 384
CHUNKS = 3
FIRST = (0, 2, 5, 7)
OFFSETS = (0, 256, 640, 896)
WIDTHS = (256, 384, 256, 384)
ROWS = 256
HEADS = 4
LOCAL = HEADS * HEAD_DIM
f32, bf16 = jnp.float32, jnp.bfloat16


def coords():
    r, m = lax.axis_index("req"), lax.axis_index("mlp")
    return r, m, lax.div(r, GROUP), lax.rem(lax.div(r, NC), NY), lax.rem(r, NC)


def at(z, y, c, m):
    return (z * GROUP + y * NC + c, m)


def send(src, dst, send_sem, recv_sem, device):
    copy = pltpu.make_async_remote_copy(
        src_ref=src,
        dst_ref=dst,
        send_sem=send_sem,
        recv_sem=recv_sem,
        device_id=device,
        device_id_type=MESH,
    )
    copy.start()
    return copy


def arrival(dst, send_sem, recv_sem, device):
    pltpu.make_async_remote_copy(
        src_ref=dst,
        dst_ref=dst,
        send_sem=send_sem,
        recv_sem=recv_sem,
        device_id=device,
        device_id_type=MESH,
    ).wait_recv()


def departure(src, send_sem, recv_sem, device):
    pltpu.make_async_remote_copy(
        src_ref=src,
        dst_ref=src,
        send_sem=send_sem,
        recv_sem=recv_sem,
        device_id=device,
        device_id_type=MESH,
    ).wait_send()


def iota(shape, dim):
    return lax.broadcasted_iota(jnp.int32, shape, dim)


def hot(mask):
    return jnp.where(mask, 1.0, 0.0).astype(bf16)


def mm(a, b):
    return jnp.dot(a, b, preferred_element_type=f32)


def mm_t(a, b):
    return lax.dot_general(a, b, (((1,), (1,)), ((), ())), preferred_element_type=f32)


def norm(x, gain):
    scale = lax.rsqrt(jnp.mean(x * x, -1, keepdims=True) + eps)
    return (x * scale * gain).astype(bf16)


def swap_order(rows_first):
    a, b = iota((ROWS, ROWS), 0), iota((ROWS, ROWS), 1)
    if not rows_first:
        a, b = b, a
    other = (a & 7) * 32 + ((a >> 3) & 1) * 16 + (a >> 4)
    return hot(other == b)


class Ring:
    CHUNKS = 5
    ROWS = BLOCK // CHUNKS

    def __init__(self, full, own, c, place, near, sibling, sems):
        self.full, self.own, self.c, self.place = full, own, c, place
        self.near, self.sibling = near, sibling
        self.chunk_ssem, self.chunk_rsem, self.block_ssem, self.block_rsem = sems

    def block(self, half, number):
        return self.full.at[half, lax.rem(number + 2 * NZ, NZ)]

    def chunk(self, ref, k):
        return ref.at[pl.ds(k * self.ROWS, self.ROWS)]

    def push(self, part, slot, device):
        send(part, part, self.chunk_ssem, self.chunk_rsem.at[slot], device)

    def hand(self, block):
        send(block, block, self.block_ssem, self.block_rsem, self.sibling)

    def start(self, value):
        self.full[self.c, self.place] = value
        own = self.block(self.c, self.place)
        for k in range(self.CHUNKS):
            for side in range(2):
                part = self.chunk(own, k)
                self.push(part, side * 20 + k, self.near[side])
        self.hand(own)

    def step(self, s):
        sides = (-1, 1)
        for k in range(self.CHUNKS):
            for side in range(2):
                if s == 3 and (k < 3) != (side == 0):
                    continue
                slot = side * 20 + s * 5 + k
                part = self.chunk(self.block(self.c, self.place + sides[side] * (1 + s)), k)
                arrival(part, self.chunk_ssem, self.chunk_rsem.at[slot], self.near[side])
                if s < 2 or (s == 2 and (k < 3) == (side == 0)):
                    self.push(part, slot + 5, self.near[side])
        for side in range(2):
            if s < 3 or side == 0:
                self.hand(self.block(self.c, self.place + sides[side] * (1 + s)))

    def finish(self):
        arrival(self.full.at[1 - self.c], self.block_ssem, self.block_rsem, self.sibling)

    def drain(self):
        departure(self.full.at[0, pl.ds(0, 7)], self.chunk_ssem, self.block_rsem, self.sibling)
        departure(self.full.at[0], self.block_ssem, self.block_rsem, self.sibling)


def to_col(row):
    eye = iota((128, 128), 0) == iota((128, 128), 1)
    return jnp.sum(jnp.where(eye, row.astype(f32), 0.0), -1, keepdims=True)


class Pairs:
    def __init__(self, c, sibling, turn, back, device, ssem, rsem, cores=NC):
        self.c, self.sibling, self.turn, self.back = c, sibling, turn, back
        self.device, self.ssem, self.rsem, self.cores = device, ssem, rsem, cores

    def spans(self):
        for d in range(1, 8):
            for k in range(self.cores):
                yield d, k, (self.c if k == 0 else 1 - self.c)

    def send(self, pick, dst, own, distances=range(8)):
        for d, k, h in self.spans():
            if d not in distances:
                continue
            to = self.turn[d]
            send(pick(to, h), dst, self.ssem, self.rsem, self.device(to, h))
        if self.cores == 2 and 0 in distances:
            send(pick(own, 1 - self.c), dst, self.ssem, self.rsem, self.sibling)

    def wait(self, whole):
        arrival(whole, self.ssem, self.rsem, self.sibling)

    def drain(self, whole):
        departure(whole, self.ssem, self.rsem, self.sibling)


def kernel(
    image_pos,
    text_len,
    vis_gain,
    attn_gain,
    wa_hbm,
    wb_hbm,
    dest_hbm,
    owner_hbm,
    row_hbm,
    place_hbm,
    patch_hbm,
    held_hbm,
    text_hbm,
    keys_hbm,
    values_hbm,
    result,
    wa,
    wb,
    small,
    dense,
    patch,
    held,
    text,
    keys,
    values,
    piece,
    stage_a,
    stage_b,
    full_a,
    full_b,
    idx,
    idx_stage,
    idx_own,
    table,
    order,
    ordered,
    normed,
    turned_cols,
    part,
    parts,
    picked_i,
    hop_i,
    turned_i,
    image,
    picked_h,
    hop_h,
    turned_h,
    hop_back,
    held_in,
    rows,
    mixed,
    product,
    shares,
    others,
    local,
    snd,
    rcv,
    chunk_a,
    chunk_b,
):
    r, m, z, y, c = coords()
    yc = y * NC + c
    sibling = at(z, y, 1 - c, m)
    planes = [(r, lax.rem(m + d, NX)) for d in range(NX)]
    back_m = [lax.rem(m + NX - d, NX) for d in range(NX)]
    turn_y = [lax.rem(y + d, NY) for d in range(NY)]
    turn_z = [lax.rem(z + d, NZ) for d in range(NZ)]
    back_y = [lax.rem(y + NY - d, NY) for d in range(NY)]
    back_z = [lax.rem(z + NZ - d, NZ) for d in range(NZ)]

    loads = {}
    for number, (name, src, dst) in enumerate(
        (
            ("wa", wa_hbm, wa),
            ("wb", wb_hbm, wb),
            ("dest", dest_hbm, small.at[0]),
            ("owner", owner_hbm, small.at[1]),
            ("row", row_hbm, small.at[2]),
            ("place", place_hbm, small.at[3]),
            ("patch", patch_hbm, patch),
            ("held", held_hbm, held),
            ("text", text_hbm, text),
            ("keys", keys_hbm, keys.at[:, pl.ds(0, WIDTH)]),
            ("values", values_hbm, values.at[:, pl.ds(0, WIDTH)]),
        )
    ):
        loads[name] = pltpu.make_async_copy(src, dst, local.at[number])
        loads[name].start()

    peers = [sibling] + planes[1:]
    peers += [at(z, turn_y[d], h, m) for d in range(1, NY) for h in range(NC)]
    peers += [at(turn_z[d], y, h, m) for d in range(1, NZ) for h in range(NC)]
    barrier = pltpu.get_barrier_semaphore()
    for device in peers:
        pl.semaphore_signal(barrier, inc=1, device_id=device, device_id_type=MESH)

    def same_z(p, h):
        return at(z, p, h, m)

    def same_y(p, h):
        return at(p, y, h, m)

    for name in ("wa", "wb", "dest", "owner", "row", "place"):
        loads[name].wait()
    for n, ref in ((0, wa), (1, wb)):
        for h in range(NC):
            piece[n, h] = jnp.zeros((PIECE, HALF), bf16)
            piece[n, h, 0:SHARD, :] = ref[:, h * HALF : (h + 1) * HALF]
    dest_row, owner_row = small[0], small[1]
    idx[...] = jnp.concatenate([dest_row, owner_row * 128 + small[2], jnp.zeros((6, 128), jnp.int32)], 0)
    pl.semaphore_wait(barrier, len(peers))

    mine = pl.ds(pl.multiple_of(z * 8, 8), 8)
    idx_stage[mine, :] = idx[...]
    for d in range(1, NZ):
        send(idx, idx_stage.at[mine], snd.at[2], rcv.at[2], same_y(turn_z[d], c))

    group = (1 - c) * z + c * y

    def spread(n, stage):
        kept = jnp.where(c == 0, piece[n, 0].astype(f32), piece[n, 1].astype(f32))
        stage[group * NC + c] = kept.astype(bf16)
        there = (1 - c) * y + c * z
        send(piece.at[n, 1 - c], stage.at[there * NC + c], snd.at[n], rcv.at[n], sibling)
        for d in range(1, 8):
            send(piece.at[n, 0], stage.at[z * NC + c], snd.at[n], rcv.at[n], same_y(turn_z[d], 0))
            send(piece.at[n, 1], stage.at[y * NC + c], snd.at[n], rcv.at[n], same_z(turn_y[d], 1))

    def gathered(n, stage):
        arrival(stage.at[pl.ds(0, GROUP - 1)], snd.at[n], rcv.at[n], sibling)
        return mm(dense[...], stage[...].reshape(GROUP * PIECE, HALF)).astype(bf16)

    spread(0, stage_a)
    spread(1, stage_b)

    loads["patch"].wait()
    xn = norm(patch[...].astype(f32), vis_gain[...].reshape(1, WIDTH))
    j = iota((1, WIDTH), 1)
    source = lax.div(lax.rem(j, 160), 20) * 160 + lax.div(j, 160) * 20 + lax.rem(j, 20)
    for b in range(5):
        span = slice(b * 256, (b + 1) * 256)
        order[span, :] = hot(iota((256, WIDTH), 0) + b * 256 == source)
    normed[0:128, :] = xn
    turned_cols[...] = mm(xn, order[...]).astype(bf16)
    k = iota((BLOCK, 1), 0)
    dense[...] = hot(iota((BLOCK, GROUP * PIECE), 1) == lax.div(k, SHARD) * PIECE + lax.rem(k, SHARD))

    arrival(idx_stage.at[pl.ds(0, 56)], snd.at[2], rcv.at[2], sibling)
    for which in range(2):
        idx_own[which] = idx_stage[pl.ds(which, NZ, stride=8), :]
    place = (1 - c) * y + c * z

    def ring_device(p):
        return ((1 - c) * (z * GROUP + p * NC) + c * (p * GROUP + y * NC + 1), m)

    near = [ring_device(lax.rem(place + 1, 8)), ring_device(lax.rem(place + 7, 8))]
    ring_a = Ring(full_a, None, c, place, near, sibling, (snd.at[22], chunk_a, snd.at[24], rcv.at[22]))
    ring_b = Ring(full_b, None, c, place, near, sibling, (snd.at[23], chunk_b, snd.at[25], rcv.at[23]))
    tables = []
    for n in range(2):
        table[n, yc] = idx_own[n]
        tables.append(Pairs(c, sibling, turn_y, back_y, same_z, snd.at[3 + n], rcv.at[3 + n]))
    tables[1].send(lambda p, h: idx_own.at[1], table.at[1, yc], y)
    ring_a.start(gathered(0, stage_a))
    ring_a.step(0)

    tables[1].wait(table.at[1, pl.ds(0, 15)])
    code = table[1]
    asked = (code >> 7) == r
    row = (code & 127).astype(f32)
    lane = iota((GROUP, NZ, 128), 2).astype(f32)
    first = jnp.min(jnp.where(asked, lane, 1000.0), -1, keepdims=True)
    want0 = jnp.sum(jnp.where(asked & (lane == first), row, 0.0), -1, keepdims=True)
    want1 = jnp.sum(jnp.where(asked, row, 0.0), -1, keepdims=True) - want0
    pick0 = jnp.where(lane == want0, 1.0, 0.0)
    pick1 = jnp.where(lane == want1, 1.0, 0.0)
    pick = jnp.concatenate([pick0, pick1], 1).reshape(ROWS, 128).astype(bf16)
    base = pl.multiple_of(m * 320 - lax.rem(m, 2) * 64, 128)
    loads["held"].wait()
    picked_h[...] = mm(pick, held[:, pl.ds(base, WINDOW)]).astype(bf16).reshape(GROUP, 16, WINDOW)
    hop_h[yc] = picked_h[yc]
    held_y = Pairs(c, sibling, turn_y, back_y, same_z, snd.at[5], rcv.at[5])
    for step, distances in ((1, (0, 1, 2)), (2, (3, 4, 5)), (3, (6, 7))):
        held_y.send(lambda p, h: picked_h.at[p * NC + h], hop_h.at[yc], y, distances)
        ring_a.step(step)
    ring_b.start(gathered(1, stage_b))

    ring_a.finish()
    left = mm(turned_cols[...], full_a[0].reshape(WIDTH, HALF))
    for b in range(5):
        part[b] = left[:, b * 128 : (b + 1) * 128]
    right = mm(normed[0:128, :], full_a[1].reshape(WIDTH, HALF))
    for b in range(5):
        part[5 + b] = right[:, b * 128 : (b + 1) * 128]
    for k in range(CHUNKS):
        for d in range(1, NX):
            src = part.at[lax.div(planes[d][1] * 5, 2) + k]
            send(src, parts.at[m, k], snd.at[13 + k], rcv.at[13 + k], planes[d])

    dest_col = to_col(dest_row)
    earlier = (dest_col == dest_row.astype(f32)) & (iota((128, 128), 0) < iota((128, 128), 1))
    rank = jnp.sum(jnp.where(earlier, 1.0, 0.0), 0, keepdims=True)
    q = iota((ROWS, 128), 0)
    target = (q >> 5) * 16 + (q & 15)
    slot = ((q >> 4) & 1).astype(f32)
    choose = hot((dest_row == target) & (rank == slot))
    turn = swap_order(True)
    image_z = [Pairs(c, sibling, turn_z, back_z, same_y, snd.at[7 + k], rcv.at[7 + k], 1) for k in range(CHUNKS)]
    image_y = [Pairs(c, sibling, turn_y, back_y, same_z, snd.at[10 + k], rcv.at[10 + k]) for k in range(CHUNKS)]

    def summed_over_planes(k):
        arrival(parts.at[0], snd.at[13 + k], rcv.at[13 + k], sibling)
        total = part[lax.div(m * 5, 2) + k]
        for d in range(1, NX):
            total = total + parts[back_m[d], k]
        picked_i[k] = mm(choose, total.astype(bf16)).astype(bf16).reshape(NZ, 32, 128)
        hop_i[k, z] = picked_i[k, z]
        image_z[k].send(lambda p, h: picked_i.at[k, p], hop_i.at[k, z], z)

    def along_y(k):
        image_z[k].wait(hop_i.at[k, pl.ds(0, 7)])
        turned_i[k] = mm(turn, hop_i[k].reshape(ROWS, 128)).astype(bf16).reshape(GROUP, 16, 128)
        image[m, k, yc] = turned_i[k, yc]
        image_y[k].send(lambda p, h: turned_i.at[k, p * NC + h], image.at[m, k, yc], y)

    def over_planes(k):
        image_y[k].wait(image.at[m, k, pl.ds(0, 15)])
        for d in range(1, NX):
            own = image.at[m, k]
            send(own, own, snd.at[16 + k], rcv.at[16 + k], planes[d])

    owner_col = to_col(owner_row)
    same = (owner_col == owner_row.astype(f32)) & (iota((128, 128), 1) < iota((128, 128), 0))
    rank = jnp.sum(jnp.where(same, 1.0, 0.0), -1, keepdims=True).astype(jnp.int32)
    owner = owner_col.astype(jnp.int32)
    spot = (owner >> 4) * 32 + rank * 16 + (owner & 15)
    fetch = hot(spot == iota((128, ROWS), 1))
    held_y.wait(hop_h.at[pl.ds(0, 15)])
    back = mm(swap_order(False), hop_h[...].reshape(ROWS, WINDOW)).astype(bf16)
    turned_h[...] = back.reshape(NZ, 32, WINDOW)
    hop_back[z] = turned_h[z]
    held_z = Pairs(c, sibling, turn_z, back_z, same_y, snd.at[6], rcv.at[6], 1)
    held_z.send(lambda p, h: turned_h.at[p], hop_back.at[z], z)
    ring_b.step(0)
    summed_over_planes(0)
    summed_over_planes(1)
    ring_b.step(1)
    along_y(0)
    summed_over_planes(2)
    held_z.wait(hop_back.at[pl.ds(0, 7)])
    held_in[m] = mm(fetch, hop_back[...].reshape(ROWS, WINDOW)).astype(bf16)
    for d in range(1, NX):
        send(held_in.at[m], held_in.at[m], snd.at[19], rcv.at[19], planes[d])
    ring_b.step(2)
    along_y(1)
    ring_b.step(3)
    over_planes(0)
    along_y(2)
    tables[0].send(lambda p, h: idx_own.at[0], table.at[0, yc], y)
    over_planes(1)
    ring_b.finish()
    over_planes(2)
    for b in range(5):
        span = slice(b * 256, (b + 1) * 256)
        ordered[span, :] = mm(order[span, :], full_b[0].reshape(WIDTH, HALF)).astype(bf16)

    gain = attn_gain[...].reshape(1, WIDTH)
    arrival(held_in.at[pl.ds(0, 3)], snd.at[19], rcv.at[19], sibling)
    for b in range(NX):
        o, w = OFFSETS[b], WIDTHS[b]
        rows[0:128, o : o + w] = held_in[b][:, 0:w].astype(f32)
    eye = hot(iota((LOCAL, LOCAL), 0) == iota((LOCAL, LOCAL), 1))

    def keys_and_values(count):
        xk = mm(normed[0:count, :], ordered[:, 256:640])
        xv = mm(normed[0:count, :], full_b[1].reshape(WIDTH, HALF)[:, 256:640])
        return (
            mm_t(eye, xk.astype(bf16)[:, 64:384]).astype(bf16),
            mm_t(eye, xv.astype(bf16)[:, 64:384]).astype(bf16),
        )

    normed[0:128, :] = norm(rows[0:128, :], gain)
    fresh = keys_and_values(128)
    loads["keys"].wait()
    loads["values"].wait()
    place_col = to_col(small[3]).astype(jnp.int32)
    for b in range(5):
        span = slice(b * 256, (b + 1) * 256)
        match = place_col == iota((128, 256), 1) + b * 256
        put = hot(match)
        hit = jnp.sum(jnp.where(match, 1.0, 0.0), 0, keepdims=True) > 0.0
        for cached, new in ((keys, fresh[0]), (values, fresh[1])):
            cached[:, span] = jnp.where(hit, mm(new, put), cached[:, span].astype(f32)).astype(bf16)

    tables[0].wait(table.at[0, pl.ds(0, 15)])
    named = hot(table[0].reshape(128, 128) == r)
    counts = mm_t(jnp.ones((8, 128), bf16), named)
    s0, s1 = iota((128, 128), 0), iota((128, 128), 1)
    ahead = hot((s0 & 7) * 16 + (s0 >> 3) < (s1 & 7) * 16 + (s1 >> 3))
    before = mm(counts.astype(bf16), ahead)
    s, a = iota((128, ROWS), 0), iota((128, ROWS), 1)
    widen = hot(((s >> 3) == (a >> 4)) & ((s & 7) == (a & 7)))
    counts_a = mm(counts.astype(bf16), widen)[0:1]
    before_a = mm(before.astype(bf16), widen)[0:1]
    slot = ((iota((1, ROWS), 1) >> 3) & 1).astype(f32)
    number = jnp.sum(counts[0:1], -1, keepdims=True)
    wanted = jnp.full((1, 1), image_pos[0], jnp.int32).astype(f32)
    start = jnp.minimum(wanted, ROWS - number)
    length = jnp.minimum(float(ROWS), jnp.full((1, 1), text_len[0], jnp.int32).astype(f32) + number)
    q = iota((ROWS, ROWS), 0).astype(f32)
    t = iota((ROWS, ROWS), 1).astype(f32)
    choose = hot((before_a + slot == q - start) & (counts_a > slot))
    take = hot(((q < start) & (t == q)) | ((q >= start + number) & (t == q - number)))
    loads["text"].wait()
    for b in range(NX):
        o, w = OFFSETS[b], WIDTHS[b]
        rows[:, o : o + w] = mm(take, text[:, o : o + w])
    for k in range(CHUNKS):
        arrival(image.at[0], snd.at[16 + k], rcv.at[16 + k], sibling)
        for b in range(NX):
            if k * 128 < WIDTHS[b]:
                lanes = slice((FIRST[b] + k) * 128, (FIRST[b] + k + 1) * 128)
                rows[:, lanes] += mm(choose, image[b, k].reshape(ROWS, 128))

    normed[...] = norm(rows[...], gain)
    queries = mm(normed[...], ordered[:, 0:384]).astype(bf16)
    new_keys, new_values = keys_and_values(ROWS)
    keys[:, WIDTH:] = new_keys
    values[:, WIDTH:] = new_values

    factor = HEAD_DIM ** (-0.5) * float(np.log2(np.e))
    for i in range(2):
        span = slice(i * 128, (i + 1) * 128)
        count = 128 * (i + 1)
        qi = iota((128, count), 0) + i * 128
        ti = iota((128, count), 1)
        seen = (ti <= qi) & (ti.astype(f32) < length)
        live = (iota((HEAD_DIM, 128), 1) + i * 128).astype(f32) < length
        for h in range(HEADS):
            lanes = slice(h * HEAD_DIM, (h + 1) * HEAD_DIM)
            head = queries[span, lanes]
            old = mm(head, keys[lanes, 0:WIDTH])
            new = jnp.where(seen, mm(head, keys[lanes, WIDTH : WIDTH + count]), big_negative)
            highest = jnp.maximum(jnp.max(old, -1, keepdims=True), jnp.max(new, -1, keepdims=True))
            old = jnp.exp2((old - highest) * factor)
            new = jnp.exp2((new - highest) * factor)
            inverse = 1.0 / (jnp.sum(old, -1, keepdims=True) + jnp.sum(new, -1, keepdims=True))
            old, new = (old * inverse).astype(bf16), (new * inverse).astype(bf16)
            summed = mm_t(values[lanes, 0:WIDTH], old) + mm_t(values[lanes, WIDTH : WIDTH + count], new)
            mixed[i, lanes, :] = jnp.where(live, summed, 0.0).astype(bf16)
        terms = mm(full_b[1].reshape(WIDTH, HALF)[:, 0:LOCAL], mixed[i])
        product[i] = terms.reshape(NX, LOCAL, 128)
        shares[i] = terms.astype(bf16).reshape(NX, LOCAL, 128)
        for d in range(1, NX):
            src, dst = shares.at[i, planes[d][1]], others.at[i, m]
            send(src, dst, snd.at[20 + i], rcv.at[20 + i], planes[d])

    for i in range(2):
        arrival(others.at[i, pl.ds(0, 3)], snd.at[20 + i], rcv.at[20 + i], sibling)
        total = product[i, m]
        for d in range(1, NX):
            total = total + others[i, back_m[d]].astype(f32)
        result[:, i * 128 : (i + 1) * 128] = total.astype(bf16)
    departure(idx_stage.at[pl.ds(0, 56)], snd.at[2], rcv.at[2], sibling)
    departure(held_in.at[pl.ds(0, 3)], snd.at[19], rcv.at[19], sibling)
    for n, stage in ((0, stage_a), (1, stage_b)):
        departure(stage.at[pl.ds(0, GROUP - 1)], snd.at[n], rcv.at[n], sibling)
        tables[n].drain(table.at[n, pl.ds(0, 15)])
        departure(others.at[n, pl.ds(0, 3)], snd.at[20 + n], rcv.at[20 + n], sibling)
    held_y.drain(hop_h.at[pl.ds(0, 15)])
    held_z.drain(hop_back.at[pl.ds(0, 7)])
    for k in range(CHUNKS):
        departure(parts.at[0], snd.at[13 + k], rcv.at[13 + k], sibling)
        image_z[k].drain(hop_i.at[k, pl.ds(0, 7)])
        image_y[k].drain(turned_i.at[k, pl.ds(0, 15)])
        departure(image.at[0], snd.at[16 + k], rcv.at[16 + k], sibling)
    ring_a.drain()
    ring_b.drain()


VM = functools.partial(pl.BlockSpec, memory_space=pltpu.VMEM)
HB = functools.partial(pl.BlockSpec, memory_space=pl.ANY)
SM = functools.partial(pl.BlockSpec, memory_space=pltpu.SMEM)
SD = jax.ShapeDtypeStruct
DMA = pltpu.SemaphoreType.DMA


def local(
    patches,
    vis_gain,
    proj_weight,
    image_dest,
    image_pos,
    text_len,
    text,
    attn_gain,
    qkv_weight,
    out_weight,
    cache_keys,
    cache_values,
    held,
    held_owner,
    held_row,
    recompute_pos,
):
    wb = jnp.concatenate([qkv_weight[0], qkv_weight[1], out_weight.T, qkv_weight[2]], 1)
    V = pltpu.VMEM
    result = pl.pallas_call(
        kernel,
        out_shape=SD((LOCAL, ROWS), bf16),
        in_specs=[SM(), SM(), VM(), VM()] + [HB()] * 11,
        out_specs=VM(),
        scratch_shapes=[
            V((SHARD, WIDTH), bf16),
            V((SHARD, WIDTH), bf16),
            V((4, 1, 128), jnp.int32),
            V((BLOCK, GROUP * PIECE), bf16),
            V((128, WIDTH), bf16),
            V((128, WIDTH), bf16),
            V((ROWS, WIDTH), bf16),
            V((LOCAL, WIDTH + ROWS), bf16),
            V((LOCAL, WIDTH + ROWS), bf16),
            V((2, 2, PIECE, HALF), bf16),
            V((GROUP, PIECE, HALF), bf16),
            V((GROUP, PIECE, HALF), bf16),
            V((2, 8, BLOCK, HALF), bf16),
            V((2, 8, BLOCK, HALF), bf16),
            V((8, 128), jnp.int32),
            V((64, 128), jnp.int32),
            V((2, NZ, 128), jnp.int32),
            V((2, GROUP, NZ, 128), jnp.int32),
            V((WIDTH, WIDTH), bf16),
            V((WIDTH, HALF), bf16),
            V((ROWS, WIDTH), bf16),
            V((128, WIDTH), bf16),
            V((10, 128, 128), f32),
            V((NX, CHUNKS, 128, 128), f32),
            V((CHUNKS, NZ, 32, 128), bf16),
            V((CHUNKS, NZ, 32, 128), bf16),
            V((CHUNKS, GROUP, 16, 128), bf16),
            V((NX, CHUNKS, GROUP, 16, 128), bf16),
            V((GROUP, 16, WINDOW), bf16),
            V((GROUP, 16, WINDOW), bf16),
            V((NZ, 32, WINDOW), bf16),
            V((NZ, 32, WINDOW), bf16),
            V((NX, 128, WINDOW), bf16),
            V((ROWS, WIDTH), f32),
            V((2, LOCAL, 128), bf16),
            V((2, NX, LOCAL, 128), f32),
            V((2, NX, LOCAL, 128), bf16),
            V((2, NX, LOCAL, 128), bf16),
            DMA((11,)),
            DMA((26,)),
            DMA((24,)),
            DMA((40,)),
            DMA((40,)),
        ],
        compiler_params=pltpu.CompilerParams(
            collective_id=1, has_side_effects=True, vmem_limit_bytes=56 * 1024 * 1024
        ),
    )(
        image_pos,
        text_len,
        vis_gain,
        attn_gain,
        proj_weight[0],
        wb,
        image_dest.reshape(1, 128),
        held_owner.reshape(1, 128),
        held_row,
        recompute_pos,
        patches[:, 0],
        held,
        text[0],
        cache_keys[0].T,
        cache_values[0].T,
    )
    return result.T[None]


def solution(mesh):
    in_specs = (
        P("req", "mlp", None),
        P(),
        P("mlp", "req", None),
        P("req", None),
        P("req"),
        P("req"),
        P("req", None, None),
        P(),
        P(None, "req", "mlp"),
        P("mlp", "req"),
        P("req", None, "mlp"),
        P("req", None, "mlp"),
        P("req", None),
        P("req", None, None),
        P("req", None),
        P("req", None),
    )
    out_specs = P("req", None, "mlp")
    return jax.shard_map(local, mesh=mesh, in_specs=in_specs, out_specs=out_specs, check_vma=False)
```
